32 devices in a mesh: groups: 1, rows: 2 (over y), chans: 8 (over z, x), cols: 2 (over core).
Axes of the slice: x: 2, y: 2, z: 4, core: 2. Of those that a mesh axis runs over, the one named last changes fastest.
Arguments:
- feature_map: bfloat16 [5, 512, 32, 256], P('groups', 'chans', 'rows', 'cols'), may hold values from -6 to 6
- taps_x: bfloat16 [512, 63], P('chans'), may hold values from -0.75 to 0.75
- taps_y: bfloat16 [512, 63], P('chans'), may hold values from -0.75 to 0.75
- mix_weight: bfloat16 [512, 512], replicated, may hold values from -0.25 to 0.25
- mix_bias: bfloat16 [512], replicated, may hold values from -3 to 3
Outputs:
- section_out: bfloat16 [5, 512, 32, 256], P('groups', 'chans', 'rows', 'cols')
The draws below stay inside these ranges and needn't reach their ends.
All inputs are finite; a program needn't handle non-finite values.
Results may differ from the reference program's by a relative error of at most 0.0048.
Values may be sent and summed in bfloat16 or wider, within the bound.
A program may use at most 64 MiB of HBM per device.

```python
import jax
import jax.numpy as jnp
from jax import lax

C = 512
KERNEL_TAPS = 63
COLUMN_DILATION = 2
ROW_DILATION = 2
TILES = 5
MAP_ROWS = 32
MAP_COLUMNS = 256


def level_of(key, extent, pieces, smallest, high):
    loudness, own = 1.0, jax.random.fold_in(key, 6)
    for position, shards_of in pieces:
        heights = jnp.exp(jax.random.uniform(jax.random.fold_in(own, position), (shards_of,), jnp.float32, smallest / len(pieces), high / len(pieces)))
        loudness = loudness * jnp.repeat(heights, extent[position] // shards_of).reshape([-1 if axis == position else 1 for axis in range(len(extent))])
    return loudness


def bell_draw(stream_key, extent, spread, most, cuts=(), kind=jnp.bfloat16):
    result = spread * jax.random.normal(stream_key, extent, jnp.float32)
    if cuts:
        result = result * level_of(stream_key, extent, cuts, -0.22, 0.18)
    return jnp.clip(result, -most, most).astype(kind)


def setup_inputs(seed: int = 0, part: int = 0) -> dict:
    key_of = jax.random.split(jax.random.key(seed), 6)
    part_splits = jax.random.split(jax.random.fold_in(key_of[5], part), 6)
    return {
        "feature_map": bell_draw(part_splits[0], (TILES, C, MAP_ROWS, MAP_COLUMNS), 1.0, 6.0, ((1, 8), (2, 2), (3, 2))),
        "taps_x": bell_draw(key_of[1], (C, KERNEL_TAPS), KERNEL_TAPS ** -0.5, 0.75, ((0, 8),)),
        "taps_y": bell_draw(key_of[2], (C, KERNEL_TAPS), KERNEL_TAPS ** -0.5, 0.75, ((0, 8),)),
        "mix_weight": bell_draw(key_of[3], (C, C), C ** -0.5, 0.25),
        "mix_bias": bell_draw(key_of[4], (C,), 0.5, 3.0),
    }


def kernel_sweep(border_padded, coefficients, dilation, axis, tally_count):
    array_shape = list(border_padded.shape)
    array_shape[axis] = tally_count
    total = jnp.zeros(tuple(array_shape), jnp.float32)
    for tap in range(coefficients.shape[-1]):
        window = lax.slice_in_dim(border_padded, tap * dilation, tap * dilation + tally_count, axis=axis)
        total = total + window.astype(jnp.float32) * coefficients[..., tap]
    return total


def reference(feature_map, taps_x, taps_y, mix_weight, mix_bias):
    column_extent = (KERNEL_TAPS // 2) * COLUMN_DILATION
    row_extent = (KERNEL_TAPS // 2) * ROW_DILATION
    column_coefficient = taps_x.astype(jnp.float32)[:, None, None, :]
    row_coefficient = taps_y.astype(jnp.float32)[:, None, None, :]
    weight_full = mix_weight.astype(jnp.float32)
    bias_full = mix_bias.astype(jnp.float32)[:, None, None]

    def one_tile(tile):
        border_padded = jnp.pad(tile, ((0, 0), (0, 0), (column_extent, column_extent)))
        column_direction = kernel_sweep(border_padded, column_coefficient, COLUMN_DILATION, 2, MAP_COLUMNS).astype(jnp.bfloat16)
        border_padded = jnp.pad(column_direction, ((0, 0), (row_extent, row_extent), (0, 0)))
        row_direction = kernel_sweep(border_padded, row_coefficient, ROW_DILATION, 1, MAP_ROWS).astype(jnp.bfloat16)
        mixed = jnp.einsum("oc,chw->ohw", weight_full, row_direction.astype(jnp.float32))
        branch = jax.nn.gelu(mixed + bias_full, approximate=True).astype(jnp.bfloat16)
        return (tile.astype(jnp.float32) + branch.astype(jnp.float32)).astype(jnp.bfloat16)

    return lax.map(one_tile, feature_map)
```

```python
import functools

import jax
import jax.numpy as jnp
from jax import lax
from jax.experimental import pallas as pl
from jax.experimental.pallas import tpu as pltpu
from jax.sharding import PartitionSpec as P

KERNEL_TAPS = 63
HALF = KERNEL_TAPS // 2
COLUMN_DILATION = 2
ROW_DILATION = 2
MESH = pl.DeviceIdType.MESH
BF16 = jnp.bfloat16
F32 = jnp.float32


def with_halo(block, sides, width):
    for axis, dim in sides:
        count = lax.axis_size(axis)
        forward = [(i, i + 1) for i in range(count - 1)]
        backward = [(target, source) for source, target in forward]
        low = lax.ppermute(
            lax.slice_in_dim(block, block.shape[dim] - width, None, axis=dim), axis, forward
        )
        high = lax.ppermute(lax.slice_in_dim(block, 0, width, axis=dim), axis, backward)
        block = jnp.concatenate([low, block, high], axis=dim)
    return block


def kernel_sweep(border_padded, coefficients, dilation, axis, tally_count):
    array_shape = list(border_padded.shape)
    array_shape[axis] = tally_count
    total = jnp.zeros(tuple(array_shape), jnp.float32)
    for tap in range(coefficients.shape[-1]):
        window = lax.slice_in_dim(
            border_padded, tap * dilation, tap * dilation + tally_count, axis=axis
        )
        total = total + window.astype(jnp.float32) * coefficients[..., tap]
    return total


def rows_pass(tall_rows, kernel):
    row_extent = KERNEL_TAPS // 2 * ROW_DILATION
    coefficients = kernel.astype(jnp.float32)[:, None, None, :]
    border_padded = jnp.pad(tall_rows, ((0, 0), (0, 0), (row_extent, row_extent), (0, 0)))
    return kernel_sweep(border_padded, coefficients, ROW_DILATION, 2, tall_rows.shape[2]).astype(
        jnp.bfloat16
    )


def x_pass(column_widened, taps_x, tally_count):
    column_coefficient = taps_x.astype(jnp.float32)[:, None, None, :]
    return kernel_sweep(column_widened, column_coefficient, COLUMN_DILATION, 3, tally_count).astype(
        jnp.bfloat16
    )


def per_device_general(feature_map, taps_x, taps_y, mix_weight, mix_bias):
    column_extent = KERNEL_TAPS // 2 * COLUMN_DILATION
    column_widened = with_halo(feature_map, (("cols", 3),), column_extent)
    column_direction = x_pass(column_widened, taps_x, feature_map.shape[3])
    tall_rows = lax.all_to_all(column_direction, "rows", split_axis=1, concat_axis=2, tiled=True)
    per_row = tall_rows.shape[1]
    offset = lax.axis_index("rows") * per_row
    kernel_part = lax.dynamic_slice_in_dim(taps_y, offset, per_row, 0)
    along_tall = rows_pass(tall_rows, kernel_part)
    row_direction = lax.all_to_all(along_tall, "rows", split_axis=2, concat_axis=1, tiled=True)
    spread = lax.all_to_all(row_direction, "chans", split_axis=2, concat_axis=1, tiled=True)
    mixed = jnp.einsum("oc,bchw->bohw", mix_weight, spread, preferred_element_type=jnp.float32)
    bias_full = mix_bias.astype(jnp.float32)[:, None, None]
    activated = jax.nn.gelu(mixed + bias_full, approximate=True).astype(jnp.bfloat16)
    branch = lax.all_to_all(activated, "chans", split_axis=1, concat_axis=2, tiled=True)
    return (feature_map.astype(jnp.float32) + branch.astype(jnp.float32)).astype(jnp.bfloat16)


def dot(a, b):
    return jnp.dot(a, b, preferred_element_type=F32)


def iota(shape, dim):
    return lax.broadcasted_iota(jnp.int32, shape, dim)


def section_kernel(
    dims,
    feat_hbm, tapx_hbm, tapy_hbm, weight_hbm, bias_hbm,
    out_ref,
    tapx_ref, tapy_ref, weight_ref, bias_ref,
    feat, whole, toep, rowmat, swap, biasb, xbuf, ybuf, gath, brch, back, mtapx, mtapy,
    loc_sem, asend, arecv, csend, crecv, dsend, drecv, tsend, trecv, seen,
):
    T, nr, nch, nco, C, CB, H, W = dims
    quads = nr * nco
    cq = CB // quads
    FH, FW = nr * H, nco * W
    nx = 2
    nz = nch // nx
    half_ch = nch // 2
    rp = H // nch
    r, ch, co = lax.axis_index("rows"), lax.axis_index("chans"), lax.axis_index("cols")
    q = r * nco + co
    z, x = ch // nx, lax.rem(ch, nx)
    half = ch // half_ch
    mirror = (nz - 1 - z) * nx + x

    def at(dr, c, dc):
        return lax.rem(r + dr, nr), c, lax.rem(co + dc, nco)

    def peer(dr, i, dc):
        return at(dr, lax.rem(ch + i, nch), dc)

    def dev(p):
        return {"rows": p[0], "chans": p[1], "cols": p[2]}

    barrier = pltpu.get_barrier_semaphore()

    def tell(sem, p):
        pl.semaphore_signal(sem, inc=1, device_id=dev(p), device_id_type=MESH)

    def along_z(sem, everyone):
        def quad_of(c):
            for dr in range(nr if everyone else 1):
                for dc in range(nco if everyone else 1):
                    tell(sem, at(dr, c, dc))

        @pl.when(z > 0)
        def _():
            quad_of(ch - nx)

        @pl.when(z < nz - 1)
        def _():
            quad_of(ch + nx)

    ends = (z > 0).astype(jnp.int32) + (z < nz - 1).astype(jnp.int32)
    over_x = z * nx + 1 - x
    along_z(barrier, True)
    for dr in range(nr):
        for dc in range(nco):
            if dr or dc:
                tell(barrier, at(dr, ch, dc))
    tell(barrier, at(0, over_x, 0))

    small = []
    for k, (src, dst) in enumerate(
        ((tapx_hbm, tapx_ref), (tapy_hbm, tapy_ref), (bias_hbm, bias_ref), (weight_hbm, weight_ref))
    ):
        c = pltpu.make_async_copy(src, dst, loc_sem.at[1 + T + k])
        c.start()
        small.append(c)
    own = pltpu.make_async_copy(feat_hbm, feat, loc_sem.at[0])
    mine = []
    for i in range(T):
        if i == 1:
            continue
        c = pltpu.make_async_copy(
            feat_hbm.at[half if i == 0 else i, pl.ds(pl.multiple_of(q * cq, cq), cq)],
            whole.at[i, r, co],
            loc_sem.at[1 + i],
        )
        c.start()
        mine.append(c)
    qs = pl.ds(pl.multiple_of(q * cq, cq), cq)

    def share(i):
        t = half if i == 0 else i
        for dr in range(nr - 1, -1, -1):
            for dc in range(nco):
                if dr == 0 and dc == 0:
                    continue
                p = at(dr, ch, dc)
                pq = p[0] * nco + p[2]
                pltpu.make_async_remote_copy(
                    src_ref=feat_hbm.at[t, pl.ds(pq * cq, cq)],
                    dst_ref=whole.at[i, r, co],
                    send_sem=asend.at[0],
                    recv_sem=arecv.at[i],
                    device_id=dev(p),
                    device_id_type=MESH,
                ).start()

    def cross():
        for dr in range(nr):
            for dc in range(nco):
                p = at(dr, mirror, dc)
                pq = p[0] * nco + p[2]
                pltpu.make_async_remote_copy(
                    src_ref=feat_hbm.at[1 - half, pl.ds(pq * cq, cq)],
                    dst_ref=whole.at[1, r, co],
                    send_sem=asend.at[1],
                    recv_sem=arecv.at[1],
                    device_id=dev(p),
                    device_id_type=MESH,
                ).start()

    def send_taps():
        for k, (src, dst) in enumerate(((tapx_ref, mtapx), (tapy_ref, mtapy))):
            pltpu.make_async_remote_copy(
                src_ref=src.at[qs, :],
                dst_ref=dst,
                send_sem=tsend.at[k],
                recv_sem=trecv.at[k],
                device_id=dev(at(0, mirror, 0)),
                device_id_type=MESH,
            ).start()

    inner = (z > 0) & (z < nz - 1)
    pl.semaphore_wait(barrier, quads - 1 + quads * ends + 1)

    along_z(seen.at[0], False)
    tell(seen.at[0], at(0, over_x, 0))

    @pl.when(inner)
    def _():
        cross()

    share(2)
    share(3)

    pl.semaphore_wait(seen.at[0], ends + 1)
    along_z(seen.at[1], False)
    own.start()
    for c in small:
        c.wait()
    pl.semaphore_wait(seen.at[1], ends)
    along_z(seen.at[2], False)

    @pl.when(jnp.logical_not(inner))
    def _():
        cross()

    share(0)
    share(4)
    send_taps()

    def prepare(n, tx, ty):
        tap = iota((KERNEL_TAPS, FW), 0)
        pos = iota((KERNEL_TAPS, FW), 1)
        d = lax.rem(HALF * COLUMN_DILATION - COLUMN_DILATION * tap + FW, FW)
        spread_x = dot(tx, (pos == d).astype(F32).astype(BF16))
        jj = iota((16, FW), 0)
        ww = iota((16, FW), 1)
        reach = HALF * COLUMN_DILATION
        for c in range(cq):
            base = jnp.broadcast_to(spread_x[c : c + 1, :], (16, FW))
            base = pltpu.roll(base, 0, 1, stride=1, stride_axis=0)
            for b in range(FW // 16):
                rolled = base if b == 0 else pltpu.roll(base, 16 * b, 1)
                delta = ww - jj - 16 * b
                keep = (delta <= reach) & (delta >= -reach)
                toep[n, c, pl.ds(16 * b, 16), :] = jnp.where(keep, rolled, 0.0).astype(BF16)

        KK = cq * FH
        tap = iota((KERNEL_TAPS, FH), 0)
        pos = iota((KERNEL_TAPS, FH), 1)
        own_channel = (iota((cq, KK), 1) // FH) == iota((cq, KK), 0)
        for h in range(FH):
            pick = (pos - h) == ROW_DILATION * (tap - HALF)
            one = dot(ty, pick.astype(F32).astype(BF16))
            tiled = jnp.concatenate([one] * cq, axis=1)
            rowmat[n, pl.ds(h * cq, cq), :] = jnp.where(own_channel, tiled, 0.0).astype(BF16)

    prepare(0, tapx_ref[qs, :], tapy_ref[qs, :])

    def prepare_mirror():
        for k, ref in enumerate((mtapx, mtapy)):
            pltpu.make_async_copy(ref, ref, trecv.at[k]).wait()
        prepare(1, mtapx[...], mtapy[...])

    def constants():
        a = iota((16 * H, 16 * H), 0)
        b = iota((16 * H, 16 * H), 1)
        swap[...] = ((a // H == lax.rem(b, 16)) & (lax.rem(a, H) == b // 16)).astype(F32).astype(BF16)
        diag = jnp.where(
            iota((C, C), 0) == iota((C, C), 1), jnp.broadcast_to(bias_ref[...].astype(F32).reshape(1, C), (C, C)), 0.0
        )
        biasb[...] = dot(diag.astype(BF16), jnp.ones((C, W), BF16))

    for c in mine:
        c.wait()
    own.wait()
    pl.semaphore_wait(seen.at[2], ends)

    def full_map(i, c):
        bands = [
            jnp.concatenate([whole[i, a, b, c] for b in range(nco)], axis=1) for a in range(nr)
        ]
        return jnp.concatenate(bands, axis=0)

    def conv(i):
        n = 1 if i == 1 else 0
        arrived = quads if i == 1 else quads - 1
        landed = whole.at[0, :, :, pl.ds(0, cq // quads * arrived)]
        pltpu.make_async_copy(landed, landed, arecv.at[i]).wait()

        @pl.loop(0, cq, unroll=4)
        def _(c):
            xbuf[pl.ds(pl.multiple_of(c * FH, FH), FH), :] = dot(full_map(i, c), toep[n, c]).astype(BF16)

        along = dot(rowmat[n], xbuf[...]).astype(BF16).reshape(FH, cq, FW)
        for k in range(nco):
            ybuf[i, k] = along[:, :, k * W : (k + 1) * W]

    def push(i):
        pair = i < 2
        group = half_ch if pair else nch
        rows = H // group
        first = 0 if pair else i * rp
        base = half * half_ch if pair else 0
        block = (mirror if i == 1 else ch) * quads + q
        chan_rows = pl.ds(pl.multiple_of(block * cq, cq), cq)
        place = lax.rem(ch, group)
        sem = crecv.at[i]

        def piece(p):
            return ybuf.at[i, p[2], pl.ds(p[0] * H + lax.rem(p[1], group) * rows, rows)]

        spot = gath.at[pl.ds(first, rows), chan_rows, :]

        def go(j, dr, dc):
            p = at(dr, base + lax.rem(place + j, group), dc)
            pltpu.make_async_remote_copy(
                src_ref=piece(p),
                dst_ref=spot,
                send_sem=csend.at[1 if pair else 0],
                recv_sem=sem,
                device_id=dev(p),
                device_id_type=MESH,
            ).start()

        @pl.loop(0, group - 1)
        def _(s):
            j = lax.rem((group // 2) * (s + 1) - 1, group - 1) + 1
            for dr in range(nr):
                for dc in range(nco):
                    go(j, dr, dc)

        for dr in range(nr):
            for dc in range(nco):
                if dr or dc:
                    go(0, dr, dc)
        pltpu.make_async_copy(piece((r, ch, co)), spot, sem).start()

    def mix(i):
        pair = i < 2
        group = half_ch if pair else nch
        rows = H // group
        first = 0 if pair else i * rp
        for n in ((0, 1) if pair else (i,)):
            got = gath.at[pl.ds(0, rows), pl.ds(0, C // 2 if pair else C), :]
            pltpu.make_async_copy(got, got, crecv.at[n]).wait()

        for k in range(rows):
            v = dot(weight_ref[...], gath[first + k]) + biasb[...]
            inner = 0.7978845608028654 * (v + 0.044715 * (v * v * v))
            brch[first + k] = (0.5 * v * (1.0 + jnp.tanh(inner))).astype(BF16)

        tile = half if pair else i

        def piece(pc):
            return brch.at[pl.ds(first, rows), pl.ds(pl.multiple_of(pc * CB, CB), CB), :]

        spot = back.at[tile, pl.ds(lax.rem(ch, group) * rows, rows)]

        @pl.loop(0, nch - 1)
        def _(s):
            p = peer(0, lax.rem((nch // 2) * (s + 1) - 1, nch - 1) + 1, 0)
            pltpu.make_async_remote_copy(
                src_ref=piece(p[1]),
                dst_ref=spot,
                send_sem=dsend,
                recv_sem=drecv.at[tile],
                device_id=dev(p),
                device_id_type=MESH,
            ).start()

        pltpu.make_async_copy(piece(ch), spot, drecv.at[tile]).start()

    def finish(t):
        pltpu.make_async_copy(back.at[t], back.at[t], drecv.at[t]).wait()
        for g in range(CB // 16):
            rows = back[t, :, g * 16 : (g + 1) * 16, :].reshape(H * 16, W)
            branch = dot(swap[...], rows).reshape(16, H, W)
            out_ref[t, g * 16 : (g + 1) * 16] = (
                feat[t, g * 16 : (g + 1) * 16].astype(F32) + branch
            ).astype(BF16)

    conv(2)
    push(2)
    constants()
    conv(3)
    push(3)
    conv(0)
    push(0)
    prepare_mirror()
    conv(1)
    push(1)
    conv(4)
    push(4)
    mix(2)
    mix(0)
    mix(3)
    finish(0)
    finish(1)
    mix(4)
    finish(2)
    finish(3)
    finish(4)

    sent = whole.at[pl.ds(0, T - 1), :, :, pl.ds(0, cq // quads * (quads - 1))]
    pltpu.make_async_copy(sent, sent, asend.at[0]).wait()
    pltpu.make_async_copy(whole.at[1], whole.at[1], asend.at[1]).wait()
    for k, ref in enumerate((mtapx, mtapy)):
        pltpu.make_async_copy(ref, ref, tsend.at[k]).wait()
    parts = nr * nch * nco
    sent = gath.at[pl.ds(2 * rp, (T - 2) * rp), pl.ds(0, C // parts * (parts - 1)), :]
    pltpu.make_async_copy(sent, sent, csend.at[0]).wait()
    parts = nr * half_ch * nco
    sent = gath.at[pl.ds(0, 2 * rp), pl.ds(0, C // parts * (parts - 1)), :]
    pltpu.make_async_copy(sent, sent, csend.at[1]).wait()
    sent = brch.at[:, pl.ds(0, C // nch * (nch - 1)), :]
    pltpu.make_async_copy(sent, sent, dsend).wait()


def per_device(mesh, feature_map, taps_x, taps_y, mix_weight, mix_bias):
    T, CB, H, W = feature_map.shape
    C = mix_weight.shape[0]
    nr, nch, nco = (mesh.shape[a] for a in ("rows", "chans", "cols"))
    quads = nr * nco
    cq = CB // quads
    rp = H // max(nch, 1)
    FH, FW = nr * H, nco * W
    dims = (T, nr, nch, nco, C, CB, H, W)
    return pl.pallas_call(
        functools.partial(section_kernel, dims),
        out_shape=jax.ShapeDtypeStruct(feature_map.shape, BF16),
        in_specs=[pl.BlockSpec(memory_space=pltpu.HBM)] * 5,
        out_specs=pl.BlockSpec(memory_space=pltpu.VMEM),
        scratch_shapes=[
            pltpu.VMEM(taps_x.shape, BF16),
            pltpu.VMEM(taps_y.shape, BF16),
            pltpu.VMEM(mix_weight.shape, BF16),
            pltpu.VMEM((C,), BF16),
            pltpu.VMEM((T, CB, H, W), BF16),
            pltpu.VMEM((T, nr, nco, cq, H, W), BF16),
            pltpu.VMEM((2, cq, FW, FW), BF16),
            pltpu.VMEM((2, FH * cq, cq * FH), BF16),
            pltpu.VMEM((16 * H, 16 * H), BF16),
            pltpu.VMEM((C, W), F32),
            pltpu.VMEM((cq * FH, FW), BF16),
            pltpu.VMEM((T, nco, FH, cq, W), BF16),
            pltpu.VMEM((T * rp, C, W), BF16),
            pltpu.VMEM((T * rp, C, W), BF16),
            pltpu.VMEM((T, H, CB, W), BF16),
            pltpu.VMEM((cq, KERNEL_TAPS), BF16),
            pltpu.VMEM((cq, KERNEL_TAPS), BF16),
            pltpu.SemaphoreType.DMA((5 + T,)),
            pltpu.SemaphoreType.DMA((2,)),
            pltpu.SemaphoreType.DMA((T,)),
            pltpu.SemaphoreType.DMA((2,)),
            pltpu.SemaphoreType.DMA((T,)),
            pltpu.SemaphoreType.DMA,
            pltpu.SemaphoreType.DMA((T,)),
            pltpu.SemaphoreType.DMA((2,)),
            pltpu.SemaphoreType.DMA((2,)),
            pltpu.SemaphoreType.REGULAR((3,)),
        ],
        compiler_params=pltpu.CompilerParams(
            collective_id=0, has_side_effects=True, vmem_limit_bytes=40 * 1024 * 1024
        ),
    )(*(pltpu.with_memory_space_constraint(v, pltpu.HBM) for v in (feature_map, taps_x, taps_y, mix_weight, mix_bias)))


def fits_kernel(mesh):
    return mesh.shape["rows"] == 2 and mesh.shape["cols"] == 2 and mesh.shape["chans"] == 8


def solution(mesh):
    body = functools.partial(per_device, mesh) if fits_kernel(mesh) else per_device_general
    return jax.shard_map(
        body,
        mesh=mesh,
        in_specs=(
            P("groups", "chans", "rows", "cols"),
            P("chans", None),
            P("chans", None),
            P(),
            P(),
        ),
        out_specs=P("groups", "chans", "rows", "cols"),
        check_vma=False,
    )
```

```python
import functools

import jax
import jax.numpy as jnp
from jax import lax
from jax.experimental import pallas as pl
from jax.experimental.pallas import tpu as pltpu
from jax.sharding import PartitionSpec as P

KERNEL_TAPS = 63
HALF = KERNEL_TAPS // 2
COLUMN_DILATION = 2
ROW_DILATION = 2
MESH = pl.DeviceIdType.MESH
BF16 = jnp.bfloat16
F32 = jnp.float32


def with_halo(block, sides, width):
    for axis, dim in sides:
        count = lax.axis_size(axis)
        forward = [(i, i + 1) for i in range(count - 1)]
        backward = [(target, source) for source, target in forward]
        low = lax.ppermute(
            lax.slice_in_dim(block, block.shape[dim] - width, None, axis=dim), axis, forward
        )
        high = lax.ppermute(lax.slice_in_dim(block, 0, width, axis=dim), axis, backward)
        block = jnp.concatenate([low, block, high], axis=dim)
    return block


def kernel_sweep(border_padded, coefficients, dilation, axis, tally_count):
    array_shape = list(border_padded.shape)
    array_shape[axis] = tally_count
    total = jnp.zeros(tuple(array_shape), jnp.float32)
    for tap in range(coefficients.shape[-1]):
        window = lax.slice_in_dim(
            border_padded, tap * dilation, tap * dilation + tally_count, axis=axis
        )
        total = total + window.astype(jnp.float32) * coefficients[..., tap]
    return total


def rows_pass(tall_rows, kernel):
    row_extent = KERNEL_TAPS // 2 * ROW_DILATION
    coefficients = kernel.astype(jnp.float32)[:, None, None, :]
    border_padded = jnp.pad(tall_rows, ((0, 0), (0, 0), (row_extent, row_extent), (0, 0)))
    return kernel_sweep(border_padded, coefficients, ROW_DILATION, 2, tall_rows.shape[2]).astype(
        jnp.bfloat16
    )


def x_pass(column_widened, taps_x, tally_count):
    column_coefficient = taps_x.astype(jnp.float32)[:, None, None, :]
    return kernel_sweep(column_widened, column_coefficient, COLUMN_DILATION, 3, tally_count).astype(
        jnp.bfloat16
    )


def per_device_general(feature_map, taps_x, taps_y, mix_weight, mix_bias):
    column_extent = KERNEL_TAPS // 2 * COLUMN_DILATION
    column_widened = with_halo(feature_map, (("cols", 3),), column_extent)
    column_direction = x_pass(column_widened, taps_x, feature_map.shape[3])
    tall_rows = lax.all_to_all(column_direction, "rows", split_axis=1, concat_axis=2, tiled=True)
    per_row = tall_rows.shape[1]
    offset = lax.axis_index("rows") * per_row
    kernel_part = lax.dynamic_slice_in_dim(taps_y, offset, per_row, 0)
    along_tall = rows_pass(tall_rows, kernel_part)
    row_direction = lax.all_to_all(along_tall, "rows", split_axis=2, concat_axis=1, tiled=True)
    spread = lax.all_to_all(row_direction, "chans", split_axis=2, concat_axis=1, tiled=True)
    mixed = jnp.einsum("oc,bchw->bohw", mix_weight, spread, preferred_element_type=jnp.float32)
    bias_full = mix_bias.astype(jnp.float32)[:, None, None]
    activated = jax.nn.gelu(mixed + bias_full, approximate=True).astype(jnp.bfloat16)
    branch = lax.all_to_all(activated, "chans", split_axis=1, concat_axis=2, tiled=True)
    return (feature_map.astype(jnp.float32) + branch.astype(jnp.float32)).astype(jnp.bfloat16)


def dot(a, b):
    return jnp.dot(a, b, preferred_element_type=F32)


def iota(shape, dim):
    return lax.broadcasted_iota(jnp.int32, shape, dim)


def section_kernel(
    dims,
    feat_hbm, tapx_hbm, tapy_hbm, weight_hbm, bias_hbm,
    out_ref,
    tapx_ref, tapy_ref, weight_ref, bias_ref,
    feat, whole, toep, rowmat, swap, biasb, xbuf, ybuf, gath, brch, back, mtapx, mtapy,
    loc_sem, asend, arecv, csend, crecv, dsend, drecv, tsend, trecv, seen, reply,
):
    T, nr, nch, nco, C, CB, H, W = dims
    quads = nr * nco
    cq = CB // quads
    FH, FW = nr * H, nco * W
    nx = 2
    nz = nch // nx
    half_ch = nch // 2
    rp = H // nch
    r, ch, co = lax.axis_index("rows"), lax.axis_index("chans"), lax.axis_index("cols")
    q = r * nco + co
    z, x = ch // nx, lax.rem(ch, nx)
    half = ch // half_ch
    mirror = (nz - 1 - z) * nx + x

    def at(dr, c, dc):
        return lax.rem(r + dr, nr), c, lax.rem(co + dc, nco)

    def across(m):
        c, step = 0, 1
        while step < nch:
            c = c + lax.rem(ch // step + m // step % 2, 2) * step
            step *= 2
        return c

    def dev(p):
        return {"rows": p[0], "chans": p[1], "cols": p[2]}

    barrier = pltpu.get_barrier_semaphore()

    def tell(sem, p):
        pl.semaphore_signal(sem, inc=1, device_id=dev(p), device_id_type=MESH)

    def along_z(sem, everyone):
        def quad_of(c):
            for dr in range(nr if everyone else 1):
                for dc in range(nco if everyone else 1):
                    tell(sem, at(dr, c, dc))

        @pl.when(z > 0)
        def _():
            quad_of(ch - nx)

        @pl.when(z < nz - 1)
        def _():
            quad_of(ch + nx)

    ends = (z > 0).astype(jnp.int32) + (z < nz - 1).astype(jnp.int32)
    over_x = z * nx + 1 - x
    def quad_members(sem, upper):
        for m in range(quads):
            @pl.when((m > q) if upper else (m < q))
            def _(m=m):
                tell(sem, (m // nco, ch, m % nco))

    def quad_at(sem, c):
        for dr in range(nr):
            for dc in range(nco):
                tell(sem, at(dr, c, dc))

    quad_members(barrier, True)

    @pl.when(z < nz - 1)
    def _():
        quad_at(barrier, ch + nx)

    @pl.when(x < nx - 1)
    def _():
        tell(barrier, at(0, over_x, 0))

    small = []
    for k, (src, dst) in enumerate(
        ((tapx_hbm, tapx_ref), (tapy_hbm, tapy_ref), (bias_hbm, bias_ref), (weight_hbm, weight_ref))
    ):
        c = pltpu.make_async_copy(src, dst, loc_sem.at[1 + T + k])
        c.start()
        small.append(c)
    own = pltpu.make_async_copy(feat_hbm, feat, loc_sem.at[0])
    mine = []
    for i in range(T):
        if i == 1:
            continue
        c = pltpu.make_async_copy(
            feat_hbm.at[half if i == 0 else i, pl.ds(pl.multiple_of(q * cq, cq), cq)],
            whole.at[i, r, co],
            loc_sem.at[1 + i],
        )
        c.start()
        mine.append(c)
    qs = pl.ds(pl.multiple_of(q * cq, cq), cq)

    def share(i):
        t = half if i == 0 else i
        for dr in range(nr - 1, -1, -1):
            for dc in range(nco):
                if dr == 0 and dc == 0:
                    continue
                p = at(dr, ch, dc)
                pq = p[0] * nco + p[2]
                pltpu.make_async_remote_copy(
                    src_ref=feat_hbm.at[t, pl.ds(pq * cq, cq)],
                    dst_ref=whole.at[i, r, co],
                    send_sem=asend.at[0],
                    recv_sem=arecv.at[i],
                    device_id=dev(p),
                    device_id_type=MESH,
                ).start()

    def cross():
        for dr in range(nr):
            for dc in range(nco):
                p = at(dr, mirror, dc)
                pq = p[0] * nco + p[2]
                pltpu.make_async_remote_copy(
                    src_ref=feat_hbm.at[1 - half, pl.ds(pq * cq, cq)],
                    dst_ref=whole.at[1, r, co],
                    send_sem=asend.at[1],
                    recv_sem=arecv.at[1],
                    device_id=dev(p),
                    device_id_type=MESH,
                ).start()

    def send_taps():
        for k, (src, dst) in enumerate(((tapx_ref, mtapx), (tapy_ref, mtapy))):
            pltpu.make_async_remote_copy(
                src_ref=src.at[qs, :],
                dst_ref=dst,
                send_sem=tsend.at[k],
                recv_sem=trecv.at[k],
                device_id=dev(at(0, mirror, 0)),
                device_id_type=MESH,
            ).start()

    inner = (z > 0) & (z < nz - 1)
    below = (z > 0).astype(jnp.int32)
    above = (z < nz - 1).astype(jnp.int32)
    def wait_some(sem, count):
        @pl.when(count > 0)
        def _():
            pl.semaphore_wait(sem, count)

    wait_some(barrier, q + quads * below + x)

    @pl.when(z > 0)
    def _():
        quad_at(reply.at[1], ch - nx)

    quad_members(reply.at[0], False)

    @pl.when(x > 0)
    def _():
        tell(reply.at[2], at(0, over_x, 0))

    @pl.when(inner & (half == 1))
    def _():
        cross()

    wait_some(reply.at[0], quads - 1 - q)
    share(2)
    share(3)
    wait_some(reply.at[1], quads * above)

    @pl.when(inner & (half == 0))
    def _():
        cross()

    wait_some(reply.at[2], nx - 1 - x)
    along_z(seen.at[0], False)
    tell(seen.at[0], at(0, over_x, 0))

    pl.semaphore_wait(seen.at[0], ends + 1)
    along_z(seen.at[1], False)
    own.start()
    for c in small:
        c.wait()
    pl.semaphore_wait(seen.at[1], ends)
    along_z(seen.at[2], False)

    @pl.when(jnp.logical_not(inner))
    def _():
        cross()

    share(0)
    share(4)
    send_taps()

    def prepare(n, tx, ty):
        tap = iota((KERNEL_TAPS, FW), 0)
        pos = iota((KERNEL_TAPS, FW), 1)
        d = lax.rem(HALF * COLUMN_DILATION - COLUMN_DILATION * tap + FW, FW)
        spread_x = dot(tx, (pos == d).astype(F32).astype(BF16))
        jj = iota((16, FW), 0)
        ww = iota((16, FW), 1)
        reach = HALF * COLUMN_DILATION
        for c in range(cq):
            base = jnp.broadcast_to(spread_x[c : c + 1, :], (16, FW))
            base = pltpu.roll(base, 0, 1, stride=1, stride_axis=0)
            for b in range(FW // 16):
                rolled = base if b == 0 else pltpu.roll(base, 16 * b, 1)
                delta = ww - jj - 16 * b
                keep = (delta <= reach) & (delta >= -reach)
                toep[n, c, pl.ds(16 * b, 16), :] = jnp.where(keep, rolled, 0.0).astype(BF16)

        KK = cq * FH
        tap = iota((KERNEL_TAPS, FH), 0)
        pos = iota((KERNEL_TAPS, FH), 1)
        own_channel = (iota((cq, KK), 1) // FH) == iota((cq, KK), 0)
        for h in range(FH):
            pick = (pos - h) == ROW_DILATION * (tap - HALF)
            one = dot(ty, pick.astype(F32).astype(BF16))
            tiled = jnp.concatenate([one] * cq, axis=1)
            rowmat[n, pl.ds(h * cq, cq), :] = jnp.where(own_channel, tiled, 0.0).astype(BF16)

    prepare(0, tapx_ref[qs, :], tapy_ref[qs, :])

    def prepare_mirror():
        for k, ref in enumerate((mtapx, mtapy)):
            pltpu.make_async_copy(ref, ref, trecv.at[k]).wait()
        prepare(1, mtapx[...], mtapy[...])

    def constants():
        a = iota((16 * H, 16 * H), 0)
        b = iota((16 * H, 16 * H), 1)
        swap[...] = ((a // H == lax.rem(b, 16)) & (lax.rem(a, H) == b // 16)).astype(F32).astype(BF16)
        diag = jnp.where(
            iota((C, C), 0) == iota((C, C), 1), jnp.broadcast_to(bias_ref[...].astype(F32).reshape(1, C), (C, C)), 0.0
        )
        biasb[...] = dot(diag.astype(BF16), jnp.ones((C, W), BF16))

    for c in mine:
        c.wait()
    own.wait()
    pl.semaphore_wait(seen.at[2], ends)

    def full_map(i, c):
        bands = [
            jnp.concatenate([whole[i, a, b, c] for b in range(nco)], axis=1) for a in range(nr)
        ]
        return jnp.concatenate(bands, axis=0)

    def conv(i):
        n = 1 if i == 1 else 0
        arrived = quads if i == 1 else quads - 1
        landed = whole.at[0, :, :, pl.ds(0, cq // quads * arrived)]
        pltpu.make_async_copy(landed, landed, arecv.at[i]).wait()

        @pl.loop(0, cq, unroll=4)
        def _(c):
            xbuf[pl.ds(pl.multiple_of(c * FH, FH), FH), :] = dot(full_map(i, c), toep[n, c]).astype(BF16)

        along = dot(rowmat[n], xbuf[...]).astype(BF16).reshape(FH, cq, FW)
        for k in range(nco):
            ybuf[i, k] = along[:, :, k * W : (k + 1) * W]

    def push(i):
        pair = i < 2
        group = half_ch if pair else nch
        rows = H // group
        first = 0 if pair else i * rp
        block = (mirror if i == 1 else ch) * quads + q
        chan_rows = pl.ds(pl.multiple_of(block * cq, cq), cq)
        sem = crecv.at[i]

        def piece(p):
            return ybuf.at[i, p[2], pl.ds(p[0] * H + lax.rem(p[1], group) * rows, rows)]

        spot = gath.at[pl.ds(first, rows), chan_rows, :]

        def go(m, dr, dc):
            p = at(dr, across(m), dc)
            pltpu.make_async_remote_copy(
                src_ref=piece(p),
                dst_ref=spot,
                send_sem=csend.at[1 if pair else 0],
                recv_sem=sem,
                device_id=dev(p),
                device_id_type=MESH,
            ).start()

        for m in (4, 1, 5, 2, 6, 3, 7):
            if m >= group:
                continue
            for dr in range(nr):
                for dc in range(nco):
                    go(m, dr, dc)

        for dr in range(nr):
            for dc in range(nco):
                if dr or dc:
                    go(0, dr, dc)
        pltpu.make_async_copy(piece((r, ch, co)), spot, sem).start()

    def mix(i):
        pair = i < 2
        group = half_ch if pair else nch
        rows = H // group
        first = 0 if pair else i * rp
        for n in ((0, 1) if pair else (i,)):
            got = gath.at[pl.ds(0, rows), pl.ds(0, C // 2 if pair else C), :]
            pltpu.make_async_copy(got, got, crecv.at[n]).wait()

        for k in range(rows):
            v = dot(weight_ref[...], gath[first + k]) + biasb[...]
            inner = 0.7978845608028654 * (v + 0.044715 * (v * v * v))
            brch[first + k] = (0.5 * v * (1.0 + jnp.tanh(inner))).astype(BF16)


    def give(i, targets, own):
        pair = i < 2
        group = half_ch if pair else nch
        rows = H // group
        first = 0 if pair else i * rp
        tile = half if pair else i

        def piece(pc):
            return brch.at[pl.ds(first, rows), pl.ds(pl.multiple_of(pc * CB, CB), CB), :]

        spot = back.at[tile, pl.ds(lax.rem(ch, group) * rows, rows)]

        for c in targets:
            def send(c=c):
                pltpu.make_async_remote_copy(
                    src_ref=piece(c),
                    dst_ref=spot,
                    send_sem=dsend,
                    recv_sem=drecv.at[tile],
                    device_id=dev(at(0, c, 0)),
                    device_id_type=MESH,
                ).start()

            pl.when(ch != c)(send)

        if own:
            pltpu.make_async_copy(piece(ch), spot, drecv.at[tile]).start()

    def finish(t):
        pltpu.make_async_copy(back.at[t], back.at[t], drecv.at[t]).wait()
        for g in range(CB // 16):
            rows = back[t, :, g * 16 : (g + 1) * 16, :].reshape(H * 16, W)
            branch = dot(swap[...], rows).reshape(16, H, W)
            out_ref[t, g * 16 : (g + 1) * 16] = (
                feat[t, g * 16 : (g + 1) * 16].astype(F32) + branch
            ).astype(BF16)

    conv(2)
    push(2)
    constants()
    conv(3)
    push(3)
    conv(0)
    push(0)
    prepare_mirror()
    conv(1)
    push(1)
    conv(4)
    push(4)
    mix(2)
    give(2, (0, 1, 2, 3, 4, 5, 6, 7), True)
    mix(0)
    give(0, (0, 1, 2, 3, 4, 5, 6, 7), True)
    mix(3)
    give(3, (0, 1, 4, 5), True)
    mix(4)
    give(4, (0, 1, 4, 5), True)
    give(3, (2, 3, 6, 7), False)
    give(4, (2, 3, 6, 7), False)
    finish(0)
    finish(1)
    finish(2)
    finish(3)
    finish(4)

    sent = whole.at[pl.ds(0, T - 1), :, :, pl.ds(0, cq // quads * (quads - 1))]
    pltpu.make_async_copy(sent, sent, asend.at[0]).wait()
    pltpu.make_async_copy(whole.at[1], whole.at[1], asend.at[1]).wait()
    for k, ref in enumerate((mtapx, mtapy)):
        pltpu.make_async_copy(ref, ref, tsend.at[k]).wait()
    parts = nr * nch * nco
    sent = gath.at[pl.ds(2 * rp, (T - 2) * rp), pl.ds(0, C // parts * (parts - 1)), :]
    pltpu.make_async_copy(sent, sent, csend.at[0]).wait()
    parts = nr * half_ch * nco
    sent = gath.at[pl.ds(0, 2 * rp), pl.ds(0, C // parts * (parts - 1)), :]
    pltpu.make_async_copy(sent, sent, csend.at[1]).wait()
    sent = brch.at[:, pl.ds(0, C // nch * (nch - 1)), :]
    pltpu.make_async_copy(sent, sent, dsend).wait()


def per_device(mesh, feature_map, taps_x, taps_y, mix_weight, mix_bias):
    T, CB, H, W = feature_map.shape
    C = mix_weight.shape[0]
    nr, nch, nco = (mesh.shape[a] for a in ("rows", "chans", "cols"))
    quads = nr * nco
    cq = CB // quads
    rp = H // max(nch, 1)
    FH, FW = nr * H, nco * W
    dims = (T, nr, nch, nco, C, CB, H, W)
    return pl.pallas_call(
        functools.partial(section_kernel, dims),
        out_shape=jax.ShapeDtypeStruct(feature_map.shape, BF16),
        in_specs=[pl.BlockSpec(memory_space=pltpu.HBM)] * 5,
        out_specs=pl.BlockSpec(memory_space=pltpu.VMEM),
        scratch_shapes=[
            pltpu.VMEM(taps_x.shape, BF16),
            pltpu.VMEM(taps_y.shape, BF16),
            pltpu.VMEM(mix_weight.shape, BF16),
            pltpu.VMEM((C,), BF16),
            pltpu.VMEM((T, CB, H, W), BF16),
            pltpu.VMEM((T, nr, nco, cq, H, W), BF16),
            pltpu.VMEM((2, cq, FW, FW), BF16),
            pltpu.VMEM((2, FH * cq, cq * FH), BF16),
            pltpu.VMEM((16 * H, 16 * H), BF16),
            pltpu.VMEM((C, W), F32),
            pltpu.VMEM((cq * FH, FW), BF16),
            pltpu.VMEM((T, nco, FH, cq, W), BF16),
            pltpu.VMEM((T * rp, C, W), BF16),
            pltpu.VMEM((T * rp, C, W), BF16),
            pltpu.VMEM((T, H, CB, W), BF16),
            pltpu.VMEM((cq, KERNEL_TAPS), BF16),
            pltpu.VMEM((cq, KERNEL_TAPS), BF16),
            pltpu.SemaphoreType.DMA((5 + T,)),
            pltpu.SemaphoreType.DMA((2,)),
            pltpu.SemaphoreType.DMA((T,)),
            pltpu.SemaphoreType.DMA((2,)),
            pltpu.SemaphoreType.DMA((T,)),
            pltpu.SemaphoreType.DMA,
            pltpu.SemaphoreType.DMA((T,)),
            pltpu.SemaphoreType.DMA((2,)),
            pltpu.SemaphoreType.DMA((2,)),
            pltpu.SemaphoreType.REGULAR((3,)),
            pltpu.SemaphoreType.REGULAR((3,)),
        ],
        compiler_params=pltpu.CompilerParams(
            collective_id=0, has_side_effects=True, vmem_limit_bytes=40 * 1024 * 1024
        ),
    )(*(pltpu.with_memory_space_constraint(v, pltpu.HBM) for v in (feature_map, taps_x, taps_y, mix_weight, mix_bias)))


def fits_kernel(mesh):
    return mesh.shape["rows"] == 2 and mesh.shape["cols"] == 2 and mesh.shape["chans"] == 8


def solution(mesh):
    body = functools.partial(per_device, mesh) if fits_kernel(mesh) else per_device_general
    return jax.shard_map(
        body,
        mesh=mesh,
        in_specs=(
            P("groups", "chans", "rows", "cols"),
            P("chans", None),
            P("chans", None),
            P(),
            P(),
        ),
        out_specs=P("groups", "chans", "rows", "cols"),
        check_vma=False,
    )
```

```python
import functools

import jax
import jax.numpy as jnp
from jax import lax
from jax.experimental import pallas as pl
from jax.experimental.pallas import tpu as pltpu
from jax.sharding import PartitionSpec as P

KERNEL_TAPS = 63
HALF = KERNEL_TAPS // 2
COLUMN_DILATION = 2
ROW_DILATION = 2
MESH = pl.DeviceIdType.MESH
BF16 = jnp.bfloat16
F32 = jnp.float32


def with_halo(block, sides, width):
    for axis, dim in sides:
        count = lax.axis_size(axis)
        forward = [(i, i + 1) for i in range(count - 1)]
        backward = [(target, source) for source, target in forward]
        low = lax.ppermute(
            lax.slice_in_dim(block, block.shape[dim] - width, None, axis=dim), axis, forward
        )
        high = lax.ppermute(lax.slice_in_dim(block, 0, width, axis=dim), axis, backward)
        block = jnp.concatenate([low, block, high], axis=dim)
    return block


def kernel_sweep(border_padded, coefficients, dilation, axis, tally_count):
    array_shape = list(border_padded.shape)
    array_shape[axis] = tally_count
    total = jnp.zeros(tuple(array_shape), jnp.float32)
    for tap in range(coefficients.shape[-1]):
        window = lax.slice_in_dim(
            border_padded, tap * dilation, tap * dilation + tally_count, axis=axis
        )
        total = total + window.astype(jnp.float32) * coefficients[..., tap]
    return total


def rows_pass(tall_rows, kernel):
    row_extent = KERNEL_TAPS // 2 * ROW_DILATION
    coefficients = kernel.astype(jnp.float32)[:, None, None, :]
    border_padded = jnp.pad(tall_rows, ((0, 0), (0, 0), (row_extent, row_extent), (0, 0)))
    return kernel_sweep(border_padded, coefficients, ROW_DILATION, 2, tall_rows.shape[2]).astype(
        jnp.bfloat16
    )


def x_pass(column_widened, taps_x, tally_count):
    column_coefficient = taps_x.astype(jnp.float32)[:, None, None, :]
    return kernel_sweep(column_widened, column_coefficient, COLUMN_DILATION, 3, tally_count).astype(
        jnp.bfloat16
    )


def per_device_general(feature_map, taps_x, taps_y, mix_weight, mix_bias):
    column_extent = KERNEL_TAPS // 2 * COLUMN_DILATION
    column_widened = with_halo(feature_map, (("cols", 3),), column_extent)
    column_direction = x_pass(column_widened, taps_x, feature_map.shape[3])
    tall_rows = lax.all_to_all(column_direction, "rows", split_axis=1, concat_axis=2, tiled=True)
    per_row = tall_rows.shape[1]
    offset = lax.axis_index("rows") * per_row
    kernel_part = lax.dynamic_slice_in_dim(taps_y, offset, per_row, 0)
    along_tall = rows_pass(tall_rows, kernel_part)
    row_direction = lax.all_to_all(along_tall, "rows", split_axis=2, concat_axis=1, tiled=True)
    spread = lax.all_to_all(row_direction, "chans", split_axis=2, concat_axis=1, tiled=True)
    mixed = jnp.einsum("oc,bchw->bohw", mix_weight, spread, preferred_element_type=jnp.float32)
    bias_full = mix_bias.astype(jnp.float32)[:, None, None]
    activated = jax.nn.gelu(mixed + bias_full, approximate=True).astype(jnp.bfloat16)
    branch = lax.all_to_all(activated, "chans", split_axis=1, concat_axis=2, tiled=True)
    return (feature_map.astype(jnp.float32) + branch.astype(jnp.float32)).astype(jnp.bfloat16)


def dot(a, b):
    return jnp.dot(a, b, preferred_element_type=F32)


def iota(shape, dim):
    return lax.broadcasted_iota(jnp.int32, shape, dim)


def section_kernel(
    dims,
    feat_hbm, tapx_hbm, tapy_hbm, weight_hbm, bias_hbm,
    out_ref,
    tapx_ref, tapy_ref, weight_ref, bias_ref,
    feat, whole, toep, rowmat, swap, biasb, xbuf, ybuf, gath, brch, back, mtapx, mtapy,
    loc_sem, asend, arecv, csend, crecv, dsend, drecv, tsend, trecv, seen, reply,
):
    T, nr, nch, nco, C, CB, H, W = dims
    quads = nr * nco
    cq = CB // quads
    FH, FW = nr * H, nco * W
    nx = 2
    nz = nch // nx
    half_ch = nch // 2
    rp = H // nch
    r, ch, co = lax.axis_index("rows"), lax.axis_index("chans"), lax.axis_index("cols")
    q = r * nco + co
    z, x = ch // nx, lax.rem(ch, nx)
    half = ch // half_ch
    mirror = (nz - 1 - z) * nx + x

    def at(dr, c, dc):
        return lax.rem(r + dr, nr), c, lax.rem(co + dc, nco)

    def across(m):
        c, step = 0, 1
        while step < nch:
            c = c + lax.rem(ch // step + m // step % 2, 2) * step
            step *= 2
        return c

    def dev(p):
        return {"rows": p[0], "chans": p[1], "cols": p[2]}

    barrier = pltpu.get_barrier_semaphore()

    def tell(sem, p):
        pl.semaphore_signal(sem, inc=1, device_id=dev(p), device_id_type=MESH)

    def along_z(sem, everyone):
        def quad_of(c):
            for dr in range(nr if everyone else 1):
                for dc in range(nco if everyone else 1):
                    tell(sem, at(dr, c, dc))

        @pl.when(z > 0)
        def _():
            quad_of(ch - nx)

        @pl.when(z < nz - 1)
        def _():
            quad_of(ch + nx)

    ends = (z > 0).astype(jnp.int32) + (z < nz - 1).astype(jnp.int32)
    over_x = z * nx + 1 - x
    def quad_members(sem, upper):
        for m in range(quads):
            @pl.when((m > q) if upper else (m < q))
            def _(m=m):
                tell(sem, (m // nco, ch, m % nco))

    quad_members(barrier, True)

    def rows_from(sem, c, low, high):
        for rr in range(nr):
            @pl.when((low <= rr) & (rr <= high))
            def _(rr=rr):
                for dc in range(nco):
                    tell(sem, (rr, c, lax.rem(co + dc, nco)))

    for up in range(1, nz):
        @pl.when(z + up < nz)
        def _(up=up):
            rows_from(barrier, ch + up * nx, r, nr)

    @pl.when(x < nx - 1)
    def _():
        tell(barrier, at(0, over_x, 0))

    small = []
    for k, (src, dst) in enumerate(
        ((tapx_hbm, tapx_ref), (tapy_hbm, tapy_ref), (bias_hbm, bias_ref), (weight_hbm, weight_ref))
    ):
        c = pltpu.make_async_copy(src, dst, loc_sem.at[1 + T + k])
        c.start()
        small.append(c)
    own = pltpu.make_async_copy(feat_hbm, feat, loc_sem.at[0])
    mine = []
    for i in range(T):
        if i == 1:
            continue
        c = pltpu.make_async_copy(
            feat_hbm.at[half if i == 0 else i, pl.ds(pl.multiple_of(q * cq, cq), cq)],
            whole.at[i, r, co],
            loc_sem.at[1 + i],
        )
        c.start()
        mine.append(c)
    qs = pl.ds(pl.multiple_of(q * cq, cq), cq)

    def share(i):
        t = half if i == 0 else i
        for dr in range(nr - 1, -1, -1):
            for dc in range(nco):
                if dr == 0 and dc == 0:
                    continue
                p = at(dr, ch, dc)
                pq = p[0] * nco + p[2]
                pltpu.make_async_remote_copy(
                    src_ref=feat_hbm.at[t, pl.ds(pq * cq, cq)],
                    dst_ref=whole.at[i, r, co],
                    send_sem=asend.at[0],
                    recv_sem=arecv.at[i],
                    device_id=dev(p),
                    device_id_type=MESH,
                ).start()

    def cross(rows):
        for rr in rows:
            for dc in range(nco):
                p = rr, mirror, lax.rem(co + dc, nco)
                pltpu.make_async_remote_copy(
                    src_ref=feat_hbm.at[1 - half, pl.ds((rr * nco + p[2]) * cq, cq)],
                    dst_ref=whole.at[1, r, co],
                    send_sem=asend.at[1],
                    recv_sem=arecv.at[1],
                    device_id=dev(p),
                    device_id_type=MESH,
                ).start()

    def send_taps():
        for k, (src, dst) in enumerate(((tapx_ref, mtapx), (tapy_ref, mtapy))):
            pltpu.make_async_remote_copy(
                src_ref=src.at[qs, :],
                dst_ref=dst,
                send_sem=tsend.at[k],
                recv_sem=trecv.at[k],
                device_id=dev(at(0, mirror, 0)),
                device_id_type=MESH,
            ).start()

    above = (z < nz - 1).astype(jnp.int32)
    def wait_some(sem, count):
        @pl.when(count > 0)
        def _():
            pl.semaphore_wait(sem, count)

    wait_some(barrier, q + x + z * nco * (r + 1))

    @pl.when(half == 1)
    def _():
        rows_from(reply.at[4 + r], mirror, 0, r)

    quad_members(reply.at[0], False)

    @pl.when(z > 0)
    def _():
        tell(reply.at[1], at(0, ch - nx, 0))

    @pl.when(x > 0)
    def _():
        tell(reply.at[3], at(0, over_x, 0))

    for rr in reversed(range(nr)):
        @pl.when((half == 1) & (rr <= r))
        def _(rr=rr):
            cross((rr,))

    def prepare(n, tx, ty):
        tap = iota((KERNEL_TAPS, FW), 0)
        pos = iota((KERNEL_TAPS, FW), 1)
        d = lax.rem(HALF * COLUMN_DILATION - COLUMN_DILATION * tap + FW, FW)
        spread_x = dot(tx, (pos == d).astype(F32).astype(BF16))
        jj = iota((16, FW), 0)
        ww = iota((16, FW), 1)
        reach = HALF * COLUMN_DILATION
        for c in range(cq):
            base = jnp.broadcast_to(spread_x[c : c + 1, :], (16, FW))
            base = pltpu.roll(base, 0, 1, stride=1, stride_axis=0)
            for b in range(FW // 16):
                rolled = base if b == 0 else pltpu.roll(base, 16 * b, 1)
                delta = ww - jj - 16 * b
                keep = (delta <= reach) & (delta >= -reach)
                toep[n, c, pl.ds(16 * b, 16), :] = jnp.where(keep, rolled, 0.0).astype(BF16)

        KK = cq * FH
        tap = iota((KERNEL_TAPS, FH), 0)
        pos = iota((KERNEL_TAPS, FH), 1)
        own_channel = (iota((cq, KK), 1) // FH) == iota((cq, KK), 0)
        for h in range(FH):
            pick = (pos - h) == ROW_DILATION * (tap - HALF)
            one = dot(ty, pick.astype(F32).astype(BF16))
            tiled = jnp.concatenate([one] * cq, axis=1)
            rowmat[n, pl.ds(h * cq, cq), :] = jnp.where(own_channel, tiled, 0.0).astype(BF16)

    @pl.when(r > 0)
    def _():
        wait_some(reply.at[0], quads - 1 - q)
        share(2)
        share(3)

    for c in small:
        c.wait()
    prepare(0, tapx_ref[qs, :], tapy_ref[qs, :])

    @pl.when(r == 0)
    def _():
        pl.semaphore_wait(reply.at[0], quads - 1 - q)
        share(2)
        share(3)

    for rr in range(nr):
        @pl.when((half == 1) & (rr > r))
        def _(rr=rr):
            cross((rr,))


    @pl.when((half == 0) & (r == 0))
    def _():
        pl.semaphore_wait(reply.at[4], nco)
        cross((0,))


    @pl.when(half == 0)
    def _():
        pl.semaphore_wait(reply.at[5], nco)
        cross((1,))


    @pl.when((half == 0) & (r == 1))
    def _():
        cross((0,))

    wait_some(reply.at[1], above)
    wait_some(reply.at[3], nx - 1 - x)
    along_z(seen.at[0], False)
    tell(seen.at[0], at(0, over_x, 0))

    pl.semaphore_wait(seen.at[0], ends + 1)
    along_z(seen.at[1], False)
    own.start()
    pl.semaphore_wait(seen.at[1], ends)
    along_z(seen.at[2], False)

    share(0)
    share(4)
    send_taps()


    def prepare_mirror():
        for k, ref in enumerate((mtapx, mtapy)):
            pltpu.make_async_copy(ref, ref, trecv.at[k]).wait()
        prepare(1, mtapx[...], mtapy[...])

    def constants():
        a = iota((16 * H, 16 * H), 0)
        b = iota((16 * H, 16 * H), 1)
        swap[...] = ((a // H == lax.rem(b, 16)) & (lax.rem(a, H) == b // 16)).astype(F32).astype(BF16)
        diag = jnp.where(
            iota((C, C), 0) == iota((C, C), 1), jnp.broadcast_to(bias_ref[...].astype(F32).reshape(1, C), (C, C)), 0.0
        )
        biasb[...] = dot(diag.astype(BF16), jnp.ones((C, W), BF16))

    for c in mine:
        c.wait()
    pl.semaphore_wait(seen.at[2], ends)

    def full_map(i, c):
        bands = [
            jnp.concatenate([whole[i, a, b, c] for b in range(nco)], axis=1) for a in range(nr)
        ]
        return jnp.concatenate(bands, axis=0)

    def conv(i):
        n = 1 if i == 1 else 0
        arrived = quads if i == 1 else quads - 1
        landed = whole.at[0, :, :, pl.ds(0, cq // quads * arrived)]
        pltpu.make_async_copy(landed, landed, arecv.at[i]).wait()

        @pl.loop(0, cq, unroll=4)
        def _(c):
            xbuf[pl.ds(pl.multiple_of(c * FH, FH), FH), :] = dot(full_map(i, c), toep[n, c]).astype(BF16)

        along = dot(rowmat[n], xbuf[...]).astype(BF16).reshape(FH, cq, FW)
        for k in range(nco):
            ybuf[i, k] = along[:, :, k * W : (k + 1) * W]

    def push(i):
        pair = i < 2
        group = half_ch if pair else nch
        rows = H // group
        first = 0 if pair else i * rp
        block = (mirror if i == 1 else ch) * quads + q
        chan_rows = pl.ds(pl.multiple_of(block * cq, cq), cq)
        sem = crecv.at[i]

        def piece(p):
            return ybuf.at[i, p[2], pl.ds(p[0] * H + lax.rem(p[1], group) * rows, rows)]

        spot = gath.at[pl.ds(first, rows), chan_rows, :]

        def go(m, dr, dc):
            p = at(dr, across(m), dc)
            pltpu.make_async_remote_copy(
                src_ref=piece(p),
                dst_ref=spot,
                send_sem=csend.at[1 if pair else 0],
                recv_sem=sem,
                device_id=dev(p),
                device_id_type=MESH,
            ).start()

        for rr in range(nr):
            for m in (4, 1, 5, 2, 6, 3, 7):
                if m >= group:
                    continue
                for dc in range(nco):
                    go(m, lax.rem(rr + r, nr), dc)

        for dr in range(nr):
            for dc in range(nco):
                if dr or dc:
                    go(0, dr, dc)
        pltpu.make_async_copy(piece((r, ch, co)), spot, sem).start()

    def mix(i):
        pair = i < 2
        group = half_ch if pair else nch
        rows = H // group
        first = 0 if pair else i * rp
        for n in ((0, 1) if pair else (i,)):
            got = gath.at[pl.ds(0, rows), pl.ds(0, C // 2 if pair else C), :]
            pltpu.make_async_copy(got, got, crecv.at[n]).wait()

        for k in range(rows):
            v = dot(weight_ref[...], gath[first + k]) + biasb[...]
            inner = 0.7978845608028654 * (v + 0.044715 * (v * v * v))
            brch[first + k] = (0.5 * v * (1.0 + jnp.tanh(inner))).astype(BF16)


    def give(i, targets, own):
        pair = i < 2
        group = half_ch if pair else nch
        rows = H // group
        first = 0 if pair else i * rp
        tile = half if pair else i

        def piece(pc):
            return brch.at[pl.ds(first, rows), pl.ds(pl.multiple_of(pc * CB, CB), CB), :]

        spot = back.at[tile, pl.ds(lax.rem(ch, group) * rows, rows)]

        for c in targets:
            def send(c=c):
                pltpu.make_async_remote_copy(
                    src_ref=piece(c),
                    dst_ref=spot,
                    send_sem=dsend,
                    recv_sem=drecv.at[tile],
                    device_id=dev(at(0, c, 0)),
                    device_id_type=MESH,
                ).start()

            pl.when(ch != c)(send)

        if own:
            pltpu.make_async_copy(piece(ch), spot, drecv.at[tile]).start()

    def finish(t):
        pltpu.make_async_copy(back.at[t], back.at[t], drecv.at[t]).wait()
        for g in range(CB // 16):
            rows = back[t, :, g * 16 : (g + 1) * 16, :].reshape(H * 16, W)
            branch = dot(swap[...], rows).reshape(16, H, W)
            out_ref[t, g * 16 : (g + 1) * 16] = (
                feat[t, g * 16 : (g + 1) * 16].astype(F32) + branch
            ).astype(BF16)

    conv(2)
    push(2)
    constants()
    conv(3)
    push(3)
    conv(0)
    push(0)
    conv(4)
    push(4)
    prepare_mirror()
    conv(1)
    push(1)
    mix(2)
    give(2, (0, 1, 2, 3, 4, 5, 6, 7), True)
    mix(3)
    give(3, (0, 1, 2, 3, 4, 5, 6, 7), True)
    mix(0)
    give(0, (0, 1, 4, 5, 6, 7), True)

    @pl.when(r == 1)
    def _():
        give(0, (2, 3), False)

    mix(4)
    give(4, (0, 1, 4, 5, 6, 7), True)

    @pl.when(r == 1)
    def _():
        give(4, (2, 3), False)


    @pl.when(r == 0)
    def _():
        give(0, (2, 3), False)


    @pl.when(r == 0)
    def _():
        give(4, (2, 3), False)

    own.wait()
    finish(0)
    finish(1)
    finish(2)
    finish(3)
    finish(4)

    sent = whole.at[pl.ds(0, T - 1), :, :, pl.ds(0, cq // quads * (quads - 1))]
    pltpu.make_async_copy(sent, sent, asend.at[0]).wait()
    pltpu.make_async_copy(whole.at[1], whole.at[1], asend.at[1]).wait()
    for k, ref in enumerate((mtapx, mtapy)):
        pltpu.make_async_copy(ref, ref, tsend.at[k]).wait()
    parts = nr * nch * nco
    sent = gath.at[pl.ds(2 * rp, (T - 2) * rp), pl.ds(0, C // parts * (parts - 1)), :]
    pltpu.make_async_copy(sent, sent, csend.at[0]).wait()
    parts = nr * half_ch * nco
    sent = gath.at[pl.ds(0, 2 * rp), pl.ds(0, C // parts * (parts - 1)), :]
    pltpu.make_async_copy(sent, sent, csend.at[1]).wait()
    sent = brch.at[:, pl.ds(0, C // nch * (nch - 1)), :]
    pltpu.make_async_copy(sent, sent, dsend).wait()


def per_device(mesh, feature_map, taps_x, taps_y, mix_weight, mix_bias):
    T, CB, H, W = feature_map.shape
    C = mix_weight.shape[0]
    nr, nch, nco = (mesh.shape[a] for a in ("rows", "chans", "cols"))
    quads = nr * nco
    cq = CB // quads
    rp = H // max(nch, 1)
    FH, FW = nr * H, nco * W
    dims = (T, nr, nch, nco, C, CB, H, W)
    return pl.pallas_call(
        functools.partial(section_kernel, dims),
        out_shape=jax.ShapeDtypeStruct(feature_map.shape, BF16),
        in_specs=[pl.BlockSpec(memory_space=pltpu.HBM)] * 5,
        out_specs=pl.BlockSpec(memory_space=pltpu.VMEM),
        scratch_shapes=[
            pltpu.VMEM(taps_x.shape, BF16),
            pltpu.VMEM(taps_y.shape, BF16),
            pltpu.VMEM(mix_weight.shape, BF16),
            pltpu.VMEM((C,), BF16),
            pltpu.VMEM((T, CB, H, W), BF16),
            pltpu.VMEM((T, nr, nco, cq, H, W), BF16),
            pltpu.VMEM((2, cq, FW, FW), BF16),
            pltpu.VMEM((2, FH * cq, cq * FH), BF16),
            pltpu.VMEM((16 * H, 16 * H), BF16),
            pltpu.VMEM((C, W), F32),
            pltpu.VMEM((cq * FH, FW), BF16),
            pltpu.VMEM((T, nco, FH, cq, W), BF16),
            pltpu.VMEM((T * rp, C, W), BF16),
            pltpu.VMEM((T * rp, C, W), BF16),
            pltpu.VMEM((T, H, CB, W), BF16),
            pltpu.VMEM((cq, KERNEL_TAPS), BF16),
            pltpu.VMEM((cq, KERNEL_TAPS), BF16),
            pltpu.SemaphoreType.DMA((5 + T,)),
            pltpu.SemaphoreType.DMA((2,)),
            pltpu.SemaphoreType.DMA((T,)),
            pltpu.SemaphoreType.DMA((2,)),
            pltpu.SemaphoreType.DMA((T,)),
            pltpu.SemaphoreType.DMA,
            pltpu.SemaphoreType.DMA((T,)),
            pltpu.SemaphoreType.DMA((2,)),
            pltpu.SemaphoreType.DMA((2,)),
            pltpu.SemaphoreType.REGULAR((3,)),
            pltpu.SemaphoreType.REGULAR((4 + 2,)),
        ],
        compiler_params=pltpu.CompilerParams(
            collective_id=0, has_side_effects=True, vmem_limit_bytes=40 * 1024 * 1024
        ),
    )(*(pltpu.with_memory_space_constraint(v, pltpu.HBM) for v in (feature_map, taps_x, taps_y, mix_weight, mix_bias)))


def fits_kernel(mesh):
    return mesh.shape["rows"] == 2 and mesh.shape["cols"] == 2 and mesh.shape["chans"] == 8


def solution(mesh):
    body = functools.partial(per_device, mesh) if fits_kernel(mesh) else per_device_general
    return jax.shard_map(
        body,
        mesh=mesh,
        in_specs=(
            P("groups", "chans", "rows", "cols"),
            P("chans", None),
            P("chans", None),
            P(),
            P(),
        ),
        out_specs=P("groups", "chans", "rows", "cols"),
        check_vma=False,
    )
```

```python
import functools

import jax
import jax.numpy as jnp
from jax import lax
from jax.experimental import pallas as pl
from jax.experimental.pallas import tpu as pltpu
from jax.sharding import PartitionSpec as P

KERNEL_TAPS = 63
HALF = KERNEL_TAPS // 2
COLUMN_DILATION = 2
ROW_DILATION = 2
MESH = pl.DeviceIdType.MESH
BF16 = jnp.bfloat16
F32 = jnp.float32


def with_halo(block, sides, width):
    for axis, dim in sides:
        count = lax.axis_size(axis)
        forward = [(i, i + 1) for i in range(count - 1)]
        backward = [(target, source) for source, target in forward]
        low = lax.ppermute(
            lax.slice_in_dim(block, block.shape[dim] - width, None, axis=dim), axis, forward
        )
        high = lax.ppermute(lax.slice_in_dim(block, 0, width, axis=dim), axis, backward)
        block = jnp.concatenate([low, block, high], axis=dim)
    return block


def kernel_sweep(border_padded, coefficients, dilation, axis, tally_count):
    array_shape = list(border_padded.shape)
    array_shape[axis] = tally_count
    total = jnp.zeros(tuple(array_shape), jnp.float32)
    for tap in range(coefficients.shape[-1]):
        window = lax.slice_in_dim(
            border_padded, tap * dilation, tap * dilation + tally_count, axis=axis
        )
        total = total + window.astype(jnp.float32) * coefficients[..., tap]
    return total


def rows_pass(tall_rows, kernel):
    row_extent = KERNEL_TAPS // 2 * ROW_DILATION
    coefficients = kernel.astype(jnp.float32)[:, None, None, :]
    border_padded = jnp.pad(tall_rows, ((0, 0), (0, 0), (row_extent, row_extent), (0, 0)))
    return kernel_sweep(border_padded, coefficients, ROW_DILATION, 2, tall_rows.shape[2]).astype(
        jnp.bfloat16
    )


def x_pass(column_widened, taps_x, tally_count):
    column_coefficient = taps_x.astype(jnp.float32)[:, None, None, :]
    return kernel_sweep(column_widened, column_coefficient, COLUMN_DILATION, 3, tally_count).astype(
        jnp.bfloat16
    )


def per_device_general(feature_map, taps_x, taps_y, mix_weight, mix_bias):
    column_extent = KERNEL_TAPS // 2 * COLUMN_DILATION
    column_widened = with_halo(feature_map, (("cols", 3),), column_extent)
    column_direction = x_pass(column_widened, taps_x, feature_map.shape[3])
    tall_rows = lax.all_to_all(column_direction, "rows", split_axis=1, concat_axis=2, tiled=True)
    per_row = tall_rows.shape[1]
    offset = lax.axis_index("rows") * per_row
    kernel_part = lax.dynamic_slice_in_dim(taps_y, offset, per_row, 0)
    along_tall = rows_pass(tall_rows, kernel_part)
    row_direction = lax.all_to_all(along_tall, "rows", split_axis=2, concat_axis=1, tiled=True)
    spread = lax.all_to_all(row_direction, "chans", split_axis=2, concat_axis=1, tiled=True)
    mixed = jnp.einsum("oc,bchw->bohw", mix_weight, spread, preferred_element_type=jnp.float32)
    bias_full = mix_bias.astype(jnp.float32)[:, None, None]
    activated = jax.nn.gelu(mixed + bias_full, approximate=True).astype(jnp.bfloat16)
    branch = lax.all_to_all(activated, "chans", split_axis=1, concat_axis=2, tiled=True)
    return (feature_map.astype(jnp.float32) + branch.astype(jnp.float32)).astype(jnp.bfloat16)


def dot(a, b):
    return jnp.dot(a, b, preferred_element_type=F32)


def iota(shape, dim):
    return lax.broadcasted_iota(jnp.int32, shape, dim)


def section_kernel(
    dims,
    feat_hbm, tapx_hbm, tapy_hbm, weight_hbm, bias_hbm,
    out_ref,
    tapx_ref, tapy_ref, weight_ref, bias_ref,
    feat, whole, toep, rowmat, swap, biasb, xbuf, ybuf, gath, brch, back, mtapx, mtapy,
    loc_sem, asend, arecv, csend, crecv, dsend, drecv, tsend, trecv, seen, reply,
):
    T, nr, nch, nco, C, CB, H, W = dims
    quads = nr * nco
    cq = CB // quads
    FH, FW = nr * H, nco * W
    nx = 2
    nz = nch // nx
    half_ch = nch // 2
    rp = H // nch
    r, ch, co = lax.axis_index("rows"), lax.axis_index("chans"), lax.axis_index("cols")
    q = r * nco + co
    z, x = ch // nx, lax.rem(ch, nx)
    half = ch // half_ch
    mirror = (nz - 1 - z) * nx + x

    def at(dr, c, dc):
        return lax.rem(r + dr, nr), c, lax.rem(co + dc, nco)

    def across(m):
        c, step = 0, 1
        while step < nch:
            c = c + lax.rem(ch // step + m // step % 2, 2) * step
            step *= 2
        return c

    def dev(p):
        return {"rows": p[0], "chans": p[1], "cols": p[2]}

    barrier = pltpu.get_barrier_semaphore()

    def tell(sem, p):
        pl.semaphore_signal(sem, inc=1, device_id=dev(p), device_id_type=MESH)

    def along_z(sem, everyone):
        def quad_of(c):
            for dr in range(nr if everyone else 1):
                for dc in range(nco if everyone else 1):
                    tell(sem, at(dr, c, dc))

        @pl.when(z > 0)
        def _():
            quad_of(ch - nx)

        @pl.when(z < nz - 1)
        def _():
            quad_of(ch + nx)

    ends = (z > 0).astype(jnp.int32) + (z < nz - 1).astype(jnp.int32)
    over_x = z * nx + 1 - x
    def quad_members(sem, upper):
        for m in range(quads):
            @pl.when((m > q) if upper else (m < q))
            def _(m=m):
                tell(sem, (m // nco, ch, m % nco))

    quad_members(barrier, True)

    def rows_from(sem, c, low, high):
        for rr in range(nr):
            @pl.when((low <= rr) & (rr <= high))
            def _(rr=rr):
                for dc in range(nco):
                    tell(sem, (rr, c, lax.rem(co + dc, nco)))

    for up in range(1, nz):
        @pl.when(z + up < nz)
        def _(up=up):
            rows_from(barrier, ch + up * nx, r, nr)

    @pl.when(x < nx - 1)
    def _():
        tell(barrier, at(0, over_x, 0))

    small = []
    for k, (src, dst) in enumerate(
        ((tapx_hbm, tapx_ref), (tapy_hbm, tapy_ref), (bias_hbm, bias_ref), (weight_hbm, weight_ref))
    ):
        c = pltpu.make_async_copy(src, dst, loc_sem.at[1 + T + k])
        c.start()
        small.append(c)
    own = pltpu.make_async_copy(feat_hbm, feat, loc_sem.at[0])
    mine = []
    for i in range(T):
        if i == 1:
            continue
        c = pltpu.make_async_copy(
            feat_hbm.at[half if i == 0 else i, pl.ds(pl.multiple_of(q * cq, cq), cq)],
            whole.at[i, r, co],
            loc_sem.at[1 + i],
        )
        c.start()
        mine.append(c)
    qs = pl.ds(pl.multiple_of(q * cq, cq), cq)

    def share(i):
        t = half if i == 0 else i
        for dr in range(nr - 1, -1, -1):
            for dc in range(nco):
                if dr == 0 and dc == 0:
                    continue
                p = at(dr, ch, dc)
                pq = p[0] * nco + p[2]
                pltpu.make_async_remote_copy(
                    src_ref=feat_hbm.at[t, pl.ds(pq * cq, cq)],
                    dst_ref=whole.at[i, r, co],
                    send_sem=asend.at[0],
                    recv_sem=arecv.at[i],
                    device_id=dev(p),
                    device_id_type=MESH,
                ).start()

    def cross(rows):
        for rr in rows:
            for dc in range(nco):
                p = rr, mirror, lax.rem(co + dc, nco)
                pltpu.make_async_remote_copy(
                    src_ref=feat_hbm.at[1 - half, pl.ds((rr * nco + p[2]) * cq, cq)],
                    dst_ref=whole.at[1, r, co],
                    send_sem=asend.at[1],
                    recv_sem=arecv.at[1],
                    device_id=dev(p),
                    device_id_type=MESH,
                ).start()

    def send_taps():
        for k, (src, dst) in enumerate(((tapx_ref, mtapx), (tapy_ref, mtapy))):
            pltpu.make_async_remote_copy(
                src_ref=src.at[qs, :],
                dst_ref=dst,
                send_sem=tsend.at[k],
                recv_sem=trecv.at[k],
                device_id=dev(at(0, mirror, 0)),
                device_id_type=MESH,
            ).start()

    above = (z < nz - 1).astype(jnp.int32)
    def wait_some(sem, count):
        @pl.when(count > 0)
        def _():
            pl.semaphore_wait(sem, count)

    wait_some(barrier, q + x + z * nco * (r + 1))

    @pl.when(half == 1)
    def _():
        rows_from(reply.at[4 + r], mirror, 0, r)

    quad_members(reply.at[0], False)

    @pl.when(z > 0)
    def _():
        tell(reply.at[1], at(0, ch - nx, 0))

    @pl.when(x > 0)
    def _():
        tell(reply.at[3], at(0, over_x, 0))

    for rr in reversed(range(nr)):
        @pl.when((half == 1) & (rr <= r))
        def _(rr=rr):
            cross((rr,))

    def prepare(n, tx, ty):
        tap = iota((KERNEL_TAPS, FW), 0)
        pos = iota((KERNEL_TAPS, FW), 1)
        d = lax.rem(HALF * COLUMN_DILATION - COLUMN_DILATION * tap + FW, FW)
        spread_x = dot(tx, (pos == d).astype(F32).astype(BF16))
        jj = iota((16, FW), 0)
        ww = iota((16, FW), 1)
        reach = HALF * COLUMN_DILATION
        for c in range(cq):
            base = jnp.broadcast_to(spread_x[c : c + 1, :], (16, FW))
            base = pltpu.roll(base, 0, 1, stride=1, stride_axis=0)
            for b in range(FW // 16):
                rolled = base if b == 0 else pltpu.roll(base, 16 * b, 1)
                delta = ww - jj - 16 * b
                keep = (delta <= reach) & (delta >= -reach)
                toep[n, c, pl.ds(16 * b, 16), :] = jnp.where(keep, rolled, 0.0).astype(BF16)

        KK = cq * FH
        tap = iota((KERNEL_TAPS, FH), 0)
        pos = iota((KERNEL_TAPS, FH), 1)
        own_channel = (iota((cq, KK), 1) // FH) == iota((cq, KK), 0)
        for h in range(FH):
            pick = (pos - h) == ROW_DILATION * (tap - HALF)
            one = dot(ty, pick.astype(F32).astype(BF16))
            tiled = jnp.concatenate([one] * cq, axis=1)
            rowmat[n, pl.ds(h * cq, cq), :] = jnp.where(own_channel, tiled, 0.0).astype(BF16)

    @pl.when(r > 0)
    def _():
        wait_some(reply.at[0], quads - 1 - q)
        share(2)
        share(3)

    for c in small:
        c.wait()
    prepare(0, tapx_ref[qs, :], tapy_ref[qs, :])

    @pl.when(r == 0)
    def _():
        pl.semaphore_wait(reply.at[0], quads - 1 - q)
        share(2)
        share(3)

    for rr in range(nr):
        @pl.when((half == 1) & (rr > r))
        def _(rr=rr):
            cross((rr,))


    @pl.when((half == 0) & (r == 0))
    def _():
        pl.semaphore_wait(reply.at[4], nco)
        cross((0,))


    @pl.when(half == 0)
    def _():
        pl.semaphore_wait(reply.at[5], nco)
        cross((1,))


    @pl.when((half == 0) & (r == 1))
    def _():
        cross((0,))

    wait_some(reply.at[1], above)
    wait_some(reply.at[3], nx - 1 - x)
    along_z(seen.at[0], False)
    tell(seen.at[0], at(0, over_x, 0))

    pl.semaphore_wait(seen.at[0], ends + 1)
    along_z(seen.at[1], False)
    own.start()
    pl.semaphore_wait(seen.at[1], ends)
    along_z(seen.at[2], False)

    share(0)
    share(4)
    send_taps()


    def prepare_mirror():
        for k, ref in enumerate((mtapx, mtapy)):
            pltpu.make_async_copy(ref, ref, trecv.at[k]).wait()
        prepare(1, mtapx[...], mtapy[...])

    def constants():
        a = iota((16 * H, 16 * H), 0)
        b = iota((16 * H, 16 * H), 1)
        swap[...] = ((a // H == lax.rem(b, 16)) & (lax.rem(a, H) == b // 16)).astype(F32).astype(BF16)
        diag = jnp.where(
            iota((C, C), 0) == iota((C, C), 1), jnp.broadcast_to(bias_ref[...].astype(F32).reshape(1, C), (C, C)), 0.0
        )
        biasb[...] = dot(diag.astype(BF16), jnp.ones((C, W), BF16))

    for c in mine:
        c.wait()
    pl.semaphore_wait(seen.at[2], ends)

    def full_map(i, c):
        bands = [
            jnp.concatenate([whole[i, a, b, c] for b in range(nco)], axis=1) for a in range(nr)
        ]
        return jnp.concatenate(bands, axis=0)

    def conv(i):
        n = 1 if i == 1 else 0
        arrived = quads if i == 1 else quads - 1
        landed = whole.at[0, :, :, pl.ds(0, cq // quads * arrived)]
        pltpu.make_async_copy(landed, landed, arecv.at[i]).wait()

        @pl.loop(0, cq, unroll=4)
        def _(c):
            xbuf[pl.ds(pl.multiple_of(c * FH, FH), FH), :] = dot(full_map(i, c), toep[n, c]).astype(BF16)

        along = dot(rowmat[n], xbuf[...]).astype(BF16).reshape(FH, cq, FW)
        for k in range(nco):
            ybuf[i, k] = along[:, :, k * W : (k + 1) * W]

    def push(i):
        pair = i < 2
        group = half_ch if pair else nch
        rows = H // group
        first = 0 if pair else i * rp
        block = (mirror if i == 1 else ch) * quads + q
        chan_rows = pl.ds(pl.multiple_of(block * cq, cq), cq)
        sem = crecv.at[i]

        def piece(p):
            return ybuf.at[i, p[2], pl.ds(p[0] * H + lax.rem(p[1], group) * rows, rows)]

        spot = gath.at[pl.ds(first, rows), chan_rows, :]

        def go(m, dr, dc):
            p = at(dr, across(m), dc)
            pltpu.make_async_remote_copy(
                src_ref=piece(p),
                dst_ref=spot,
                send_sem=csend.at[1 if pair else 0],
                recv_sem=sem,
                device_id=dev(p),
                device_id_type=MESH,
            ).start()

        for rr in range(nr):
            for m in (4, 5, 6, 7, 1, 2, 3):
                if m >= group:
                    continue
                for dc in range(nco):
                    go(m, lax.rem(rr + r, nr), dc)

        for dr in range(nr):
            for dc in range(nco):
                if dr or dc:
                    go(0, dr, dc)
        pltpu.make_async_copy(piece((r, ch, co)), spot, sem).start()

    def mix(i):
        pair = i < 2
        group = half_ch if pair else nch
        rows = H // group
        first = 0 if pair else i * rp
        for n in ((0, 1) if pair else (i,)):
            got = gath.at[pl.ds(0, rows), pl.ds(0, C // 2 if pair else C), :]
            pltpu.make_async_copy(got, got, crecv.at[n]).wait()

        for k in range(rows):
            v = dot(weight_ref[...], gath[first + k]) + biasb[...]
            inner = 0.7978845608028654 * (v + 0.044715 * (v * v * v))
            brch[first + k] = (0.5 * v * (1.0 + jnp.tanh(inner))).astype(BF16)


    def give(i, targets, own):
        pair = i < 2
        group = half_ch if pair else nch
        rows = H // group
        first = 0 if pair else i * rp
        tile = half if pair else i

        def piece(pc):
            return brch.at[pl.ds(first, rows), pl.ds(pl.multiple_of(pc * CB, CB), CB), :]

        spot = back.at[tile, pl.ds(lax.rem(ch, group) * rows, rows)]

        for c in targets:
            def send(c=c):
                pltpu.make_async_remote_copy(
                    src_ref=piece(c),
                    dst_ref=spot,
                    send_sem=dsend,
                    recv_sem=drecv.at[tile],
                    device_id=dev(at(0, c, 0)),
                    device_id_type=MESH,
                ).start()

            pl.when(ch != c)(send)

        if own:
            pltpu.make_async_copy(piece(ch), spot, drecv.at[tile]).start()

    def finish(t):
        pltpu.make_async_copy(back.at[t], back.at[t], drecv.at[t]).wait()
        for g in range(CB // 16):
            rows = back[t, :, g * 16 : (g + 1) * 16, :].reshape(H * 16, W)
            branch = dot(swap[...], rows).reshape(16, H, W)
            out_ref[t, g * 16 : (g + 1) * 16] = (
                feat[t, g * 16 : (g + 1) * 16].astype(F32) + branch
            ).astype(BF16)

    conv(2)
    push(2)
    constants()
    conv(3)
    push(3)
    conv(0)
    push(0)
    conv(4)
    push(4)
    prepare_mirror()
    conv(1)
    push(1)
    mix(2)
    give(2, (0, 1, 2, 3, 4, 5, 6, 7), True)
    mix(3)
    give(3, (0, 1, 2, 3, 4, 5, 6, 7), True)
    mix(0)
    give(0, (0, 1, 4, 5, 6, 7), True)

    @pl.when(r == 1)
    def _():
        give(0, (2, 3), False)

    mix(4)
    give(4, (0, 1, 4, 5, 6, 7), True)

    @pl.when(r == 1)
    def _():
        give(4, (2, 3), False)


    @pl.when(r == 0)
    def _():
        give(0, (2, 3), False)


    @pl.when(r == 0)
    def _():
        give(4, (2, 3), False)

    own.wait()
    finish(0)
    finish(1)
    finish(2)
    finish(3)
    finish(4)

    sent = whole.at[pl.ds(0, T - 1), :, :, pl.ds(0, cq // quads * (quads - 1))]
    pltpu.make_async_copy(sent, sent, asend.at[0]).wait()
    pltpu.make_async_copy(whole.at[1], whole.at[1], asend.at[1]).wait()
    for k, ref in enumerate((mtapx, mtapy)):
        pltpu.make_async_copy(ref, ref, tsend.at[k]).wait()
    parts = nr * nch * nco
    sent = gath.at[pl.ds(2 * rp, (T - 2) * rp), pl.ds(0, C // parts * (parts - 1)), :]
    pltpu.make_async_copy(sent, sent, csend.at[0]).wait()
    parts = nr * half_ch * nco
    sent = gath.at[pl.ds(0, 2 * rp), pl.ds(0, C // parts * (parts - 1)), :]
    pltpu.make_async_copy(sent, sent, csend.at[1]).wait()
    sent = brch.at[:, pl.ds(0, C // nch * (nch - 1)), :]
    pltpu.make_async_copy(sent, sent, dsend).wait()


def per_device(mesh, feature_map, taps_x, taps_y, mix_weight, mix_bias):
    T, CB, H, W = feature_map.shape
    C = mix_weight.shape[0]
    nr, nch, nco = (mesh.shape[a] for a in ("rows", "chans", "cols"))
    quads = nr * nco
    cq = CB // quads
    rp = H // max(nch, 1)
    FH, FW = nr * H, nco * W
    dims = (T, nr, nch, nco, C, CB, H, W)
    return pl.pallas_call(
        functools.partial(section_kernel, dims),
        out_shape=jax.ShapeDtypeStruct(feature_map.shape, BF16),
        in_specs=[pl.BlockSpec(memory_space=pltpu.HBM)] * 5,
        out_specs=pl.BlockSpec(memory_space=pltpu.VMEM),
        scratch_shapes=[
            pltpu.VMEM(taps_x.shape, BF16),
            pltpu.VMEM(taps_y.shape, BF16),
            pltpu.VMEM(mix_weight.shape, BF16),
            pltpu.VMEM((C,), BF16),
            pltpu.VMEM((T, CB, H, W), BF16),
            pltpu.VMEM((T, nr, nco, cq, H, W), BF16),
            pltpu.VMEM((2, cq, FW, FW), BF16),
            pltpu.VMEM((2, FH * cq, cq * FH), BF16),
            pltpu.VMEM((16 * H, 16 * H), BF16),
            pltpu.VMEM((C, W), F32),
            pltpu.VMEM((cq * FH, FW), BF16),
            pltpu.VMEM((T, nco, FH, cq, W), BF16),
            pltpu.VMEM((T * rp, C, W), BF16),
            pltpu.VMEM((T * rp, C, W), BF16),
            pltpu.VMEM((T, H, CB, W), BF16),
            pltpu.VMEM((cq, KERNEL_TAPS), BF16),
            pltpu.VMEM((cq, KERNEL_TAPS), BF16),
            pltpu.SemaphoreType.DMA((5 + T,)),
            pltpu.SemaphoreType.DMA((2,)),
            pltpu.SemaphoreType.DMA((T,)),
            pltpu.SemaphoreType.DMA((2,)),
            pltpu.SemaphoreType.DMA((T,)),
            pltpu.SemaphoreType.DMA,
            pltpu.SemaphoreType.DMA((T,)),
            pltpu.SemaphoreType.DMA((2,)),
            pltpu.SemaphoreType.DMA((2,)),
            pltpu.SemaphoreType.REGULAR((3,)),
            pltpu.SemaphoreType.REGULAR((4 + 2,)),
        ],
        compiler_params=pltpu.CompilerParams(
            collective_id=0, has_side_effects=True, vmem_limit_bytes=40 * 1024 * 1024
        ),
    )(*(pltpu.with_memory_space_constraint(v, pltpu.HBM) for v in (feature_map, taps_x, taps_y, mix_weight, mix_bias)))


def fits_kernel(mesh):
    return mesh.shape["rows"] == 2 and mesh.shape["cols"] == 2 and mesh.shape["chans"] == 8


def solution(mesh):
    body = functools.partial(per_device, mesh) if fits_kernel(mesh) else per_device_general
    return jax.shard_map(
        body,
        mesh=mesh,
        in_specs=(
            P("groups", "chans", "rows", "cols"),
            P("chans", None),
            P("chans", None),
            P(),
            P(),
        ),
        out_specs=P("groups", "chans", "rows", "cols"),
        check_vma=False,
    )
```

```python
import functools

import jax
import jax.numpy as jnp
from jax import lax
from jax.experimental import pallas as pl
from jax.experimental.pallas import tpu as pltpu
from jax.sharding import PartitionSpec as P

KERNEL_TAPS = 63
HALF = KERNEL_TAPS // 2
COLUMN_DILATION = 2
ROW_DILATION = 2
MESH = pl.DeviceIdType.MESH
BF16 = jnp.bfloat16
F32 = jnp.float32


def with_halo(block, sides, width):
    for axis, dim in sides:
        count = lax.axis_size(axis)
        forward = [(i, i + 1) for i in range(count - 1)]
        backward = [(target, source) for source, target in forward]
        low = lax.ppermute(
            lax.slice_in_dim(block, block.shape[dim] - width, None, axis=dim), axis, forward
        )
        high = lax.ppermute(lax.slice_in_dim(block, 0, width, axis=dim), axis, backward)
        block = jnp.concatenate([low, block, high], axis=dim)
    return block


def kernel_sweep(border_padded, coefficients, dilation, axis, tally_count):
    array_shape = list(border_padded.shape)
    array_shape[axis] = tally_count
    total = jnp.zeros(tuple(array_shape), jnp.float32)
    for tap in range(coefficients.shape[-1]):
        window = lax.slice_in_dim(
            border_padded, tap * dilation, tap * dilation + tally_count, axis=axis
        )
        total = total + window.astype(jnp.float32) * coefficients[..., tap]
    return total


def rows_pass(tall_rows, kernel):
    row_extent = KERNEL_TAPS // 2 * ROW_DILATION
    coefficients = kernel.astype(jnp.float32)[:, None, None, :]
    border_padded = jnp.pad(tall_rows, ((0, 0), (0, 0), (row_extent, row_extent), (0, 0)))
    return kernel_sweep(border_padded, coefficients, ROW_DILATION, 2, tall_rows.shape[2]).astype(
        jnp.bfloat16
    )


def x_pass(column_widened, taps_x, tally_count):
    column_coefficient = taps_x.astype(jnp.float32)[:, None, None, :]
    return kernel_sweep(column_widened, column_coefficient, COLUMN_DILATION, 3, tally_count).astype(
        jnp.bfloat16
    )


def per_device_general(feature_map, taps_x, taps_y, mix_weight, mix_bias):
    column_extent = KERNEL_TAPS // 2 * COLUMN_DILATION
    column_widened = with_halo(feature_map, (("cols", 3),), column_extent)
    column_direction = x_pass(column_widened, taps_x, feature_map.shape[3])
    tall_rows = lax.all_to_all(column_direction, "rows", split_axis=1, concat_axis=2, tiled=True)
    per_row = tall_rows.shape[1]
    offset = lax.axis_index("rows") * per_row
    kernel_part = lax.dynamic_slice_in_dim(taps_y, offset, per_row, 0)
    along_tall = rows_pass(tall_rows, kernel_part)
    row_direction = lax.all_to_all(along_tall, "rows", split_axis=2, concat_axis=1, tiled=True)
    spread = lax.all_to_all(row_direction, "chans", split_axis=2, concat_axis=1, tiled=True)
    mixed = jnp.einsum("oc,bchw->bohw", mix_weight, spread, preferred_element_type=jnp.float32)
    bias_full = mix_bias.astype(jnp.float32)[:, None, None]
    activated = jax.nn.gelu(mixed + bias_full, approximate=True).astype(jnp.bfloat16)
    branch = lax.all_to_all(activated, "chans", split_axis=1, concat_axis=2, tiled=True)
    return (feature_map.astype(jnp.float32) + branch.astype(jnp.float32)).astype(jnp.bfloat16)


def dot(a, b):
    return jnp.dot(a, b, preferred_element_type=F32)


def iota(shape, dim):
    return lax.broadcasted_iota(jnp.int32, shape, dim)


def section_kernel(
    dims,
    feat_hbm, tapx_hbm, tapy_hbm, weight_hbm, bias_hbm,
    out_ref,
    tapx_ref, tapy_ref, weight_ref, bias_ref,
    feat, whole, toep, rowmat, swap, biasb, xbuf, ybuf, gath, brch, back, mtapx, mtapy,
    loc_sem, asend, arecv, csend, crecv, dsend, drecv, tsend, trecv, seen, reply,
):
    T, nr, nch, nco, C, CB, H, W = dims
    quads = nr * nco
    cq = CB // quads
    FH, FW = nr * H, nco * W
    nx = 2
    nz = nch // nx
    half_ch = nch // 2
    rp = H // nch
    r, ch, co = lax.axis_index("rows"), lax.axis_index("chans"), lax.axis_index("cols")
    q = r * nco + co
    z, x = ch // nx, lax.rem(ch, nx)
    half = ch // half_ch
    mirror = (nz - 1 - z) * nx + x

    def at(dr, c, dc):
        return lax.rem(r + dr, nr), c, lax.rem(co + dc, nco)

    def across(m):
        c, step = 0, 1
        while step < nch:
            c = c + lax.rem(ch // step + m // step % 2, 2) * step
            step *= 2
        return c

    def dev(p):
        return {"rows": p[0], "chans": p[1], "cols": p[2]}

    barrier = pltpu.get_barrier_semaphore()

    def tell(sem, p):
        pl.semaphore_signal(sem, inc=1, device_id=dev(p), device_id_type=MESH)

    def along_z(sem, everyone):
        def quad_of(c):
            for dr in range(nr if everyone else 1):
                for dc in range(nco if everyone else 1):
                    tell(sem, at(dr, c, dc))

        @pl.when(z > 0)
        def _():
            quad_of(ch - nx)

        @pl.when(z < nz - 1)
        def _():
            quad_of(ch + nx)

    ends = (z > 0).astype(jnp.int32) + (z < nz - 1).astype(jnp.int32)
    over_x = z * nx + 1 - x
    def quad_members(sem, upper):
        for m in range(quads):
            @pl.when((m > q) if upper else (m < q))
            def _(m=m):
                tell(sem, (m // nco, ch, m % nco))

    quad_members(barrier, True)

    def rows_from(sem, c, low, high):
        for rr in range(nr):
            @pl.when((low <= rr) & (rr <= high))
            def _(rr=rr):
                for dc in range(nco):
                    tell(sem, (rr, c, lax.rem(co + dc, nco)))

    for up in range(1, nz):
        @pl.when(z + up < nz)
        def _(up=up):
            rows_from(barrier, ch + up * nx, r, nr)

    @pl.when(x < nx - 1)
    def _():
        tell(barrier, at(0, over_x, 0))

    small = []
    for k, (src, dst) in enumerate(
        ((tapx_hbm, tapx_ref), (tapy_hbm, tapy_ref), (bias_hbm, bias_ref), (weight_hbm, weight_ref))
    ):
        c = pltpu.make_async_copy(src, dst, loc_sem.at[1 + T + k])
        c.start()
        small.append(c)
    own = pltpu.make_async_copy(feat_hbm, feat, loc_sem.at[0])
    mine = []
    for i in range(T):
        if i == 1:
            continue
        c = pltpu.make_async_copy(
            feat_hbm.at[half if i == 0 else i, pl.ds(pl.multiple_of(q * cq, cq), cq)],
            whole.at[i, r, co],
            loc_sem.at[1 + i],
        )
        c.start()
        mine.append(c)
    qs = pl.ds(pl.multiple_of(q * cq, cq), cq)

    def share(i):
        t = half if i == 0 else i
        for dr in range(nr - 1, -1, -1):
            for dc in range(nco):
                if dr == 0 and dc == 0:
                    continue
                p = at(dr, ch, dc)
                pq = p[0] * nco + p[2]
                pltpu.make_async_remote_copy(
                    src_ref=feat_hbm.at[t, pl.ds(pq * cq, cq)],
                    dst_ref=whole.at[i, r, co],
                    send_sem=asend.at[0],
                    recv_sem=arecv.at[i],
                    device_id=dev(p),
                    device_id_type=MESH,
                ).start()

    def cross(rows):
        for rr in rows:
            for dc in range(nco):
                p = rr, mirror, lax.rem(co + dc, nco)
                pltpu.make_async_remote_copy(
                    src_ref=feat_hbm.at[1 - half, pl.ds((rr * nco + p[2]) * cq, cq)],
                    dst_ref=whole.at[1, r, co],
                    send_sem=asend.at[1],
                    recv_sem=arecv.at[1],
                    device_id=dev(p),
                    device_id_type=MESH,
                ).start()

    def send_taps():
        for k, (src, dst) in enumerate(((tapx_ref, mtapx), (tapy_ref, mtapy))):
            pltpu.make_async_remote_copy(
                src_ref=src.at[qs, :],
                dst_ref=dst,
                send_sem=tsend.at[k],
                recv_sem=trecv.at[k],
                device_id=dev(at(0, mirror, 0)),
                device_id_type=MESH,
            ).start()

    above = (z < nz - 1).astype(jnp.int32)
    def wait_some(sem, count):
        @pl.when(count > 0)
        def _():
            pl.semaphore_wait(sem, count)

    wait_some(barrier, q + x + z * nco * (r + 1))

    @pl.when(half == 1)
    def _():
        rows_from(reply.at[4 + r], mirror, 0, r)

    quad_members(reply.at[0], False)

    @pl.when(z > 0)
    def _():
        tell(reply.at[1], at(0, ch - nx, 0))

    @pl.when(x > 0)
    def _():
        tell(reply.at[3], at(0, over_x, 0))

    for rr in reversed(range(nr)):
        @pl.when((half == 1) & (rr <= r))
        def _(rr=rr):
            cross((rr,))

    def prepare(n, tx, ty):
        tap = iota((KERNEL_TAPS, FW), 0)
        pos = iota((KERNEL_TAPS, FW), 1)
        d = lax.rem(HALF * COLUMN_DILATION - COLUMN_DILATION * tap + FW, FW)
        spread_x = dot(tx, (pos == d).astype(F32).astype(BF16))
        jj = iota((16, FW), 0)
        ww = iota((16, FW), 1)
        reach = HALF * COLUMN_DILATION
        for c in range(cq):
            base = jnp.broadcast_to(spread_x[c : c + 1, :], (16, FW))
            base = pltpu.roll(base, 0, 1, stride=1, stride_axis=0)
            for b in range(FW // 16):
                rolled = base if b == 0 else pltpu.roll(base, 16 * b, 1)
                delta = ww - jj - 16 * b
                keep = (delta <= reach) & (delta >= -reach)
                toep[n, c, pl.ds(16 * b, 16), :] = jnp.where(keep, rolled, 0.0).astype(BF16)

        KK = cq * FH
        tap = iota((KERNEL_TAPS, FH), 0)
        pos = iota((KERNEL_TAPS, FH), 1)
        own_channel = (iota((cq, KK), 1) // FH) == iota((cq, KK), 0)
        for h in range(FH):
            pick = (pos - h) == ROW_DILATION * (tap - HALF)
            one = dot(ty, pick.astype(F32).astype(BF16))
            tiled = jnp.concatenate([one] * cq, axis=1)
            rowmat[n, pl.ds(h * cq, cq), :] = jnp.where(own_channel, tiled, 0.0).astype(BF16)

    @pl.when(r > 0)
    def _():
        wait_some(reply.at[0], quads - 1 - q)
        share(2)
        share(3)

    for c in small:
        c.wait()
    prepare(0, tapx_ref[qs, :], tapy_ref[qs, :])

    @pl.when(r == 0)
    def _():
        pl.semaphore_wait(reply.at[0], quads - 1 - q)
        share(2)
        share(3)

    for rr in range(nr):
        @pl.when((half == 1) & (rr > r))
        def _(rr=rr):
            cross((rr,))


    @pl.when((half == 0) & (r == 0))
    def _():
        pl.semaphore_wait(reply.at[4], nco)
        cross((0,))


    @pl.when(half == 0)
    def _():
        pl.semaphore_wait(reply.at[5], nco)
        cross((1,))


    @pl.when((half == 0) & (r == 1))
    def _():
        cross((0,))

    wait_some(reply.at[1], above)
    wait_some(reply.at[3], nx - 1 - x)
    along_z(seen.at[0], False)
    tell(seen.at[0], at(0, over_x, 0))

    pl.semaphore_wait(seen.at[0], ends + 1)
    along_z(seen.at[1], False)
    own.start()
    pl.semaphore_wait(seen.at[1], ends)
    along_z(seen.at[2], False)

    share(0)
    share(4)
    send_taps()


    def prepare_mirror():
        for k, ref in enumerate((mtapx, mtapy)):
            pltpu.make_async_copy(ref, ref, trecv.at[k]).wait()
        prepare(1, mtapx[...], mtapy[...])

    def constants():
        a = iota((16 * H, 16 * H), 0)
        b = iota((16 * H, 16 * H), 1)
        swap[...] = ((a // H == lax.rem(b, 16)) & (lax.rem(a, H) == b // 16)).astype(F32).astype(BF16)
        diag = jnp.where(
            iota((C, C), 0) == iota((C, C), 1), jnp.broadcast_to(bias_ref[...].astype(F32).reshape(1, C), (C, C)), 0.0
        )
        biasb[...] = dot(diag.astype(BF16), jnp.ones((C, W), BF16))

    for c in mine:
        c.wait()
    pl.semaphore_wait(seen.at[2], ends)

    def full_map(i, c):
        bands = [
            jnp.concatenate([whole[i, a, b, c] for b in range(nco)], axis=1) for a in range(nr)
        ]
        return jnp.concatenate(bands, axis=0)

    def conv(i):
        n = 1 if i == 1 else 0
        arrived = quads if i == 1 else quads - 1
        landed = whole.at[0, :, :, pl.ds(0, cq // quads * arrived)]
        pltpu.make_async_copy(landed, landed, arecv.at[i]).wait()

        @pl.loop(0, cq, unroll=4)
        def _(c):
            xbuf[pl.ds(pl.multiple_of(c * FH, FH), FH), :] = dot(full_map(i, c), toep[n, c]).astype(BF16)

        along = dot(rowmat[n], xbuf[...]).astype(BF16).reshape(FH, cq, FW)
        for k in range(nco):
            ybuf[i, k] = along[:, :, k * W : (k + 1) * W]

    def push(i):
        pair = i < 2
        group = half_ch if pair else nch
        rows = H // group
        first = 0 if pair else i * rp
        block = (mirror if i == 1 else ch) * quads + q
        chan_rows = pl.ds(pl.multiple_of(block * cq, cq), cq)
        sem = crecv.at[i]

        def piece(p):
            return ybuf.at[i, p[2], pl.ds(p[0] * H + lax.rem(p[1], group) * rows, rows)]

        spot = gath.at[pl.ds(first, rows), chan_rows, :]

        def go(m, dr, dc):
            p = at(dr, across(m), dc)
            pltpu.make_async_remote_copy(
                src_ref=piece(p),
                dst_ref=spot,
                send_sem=csend.at[1 if pair else 0],
                recv_sem=sem,
                device_id=dev(p),
                device_id_type=MESH,
            ).start()

        for rr in range(nr):
            for m in (4, 1, 5, 2, 6, 3, 7):
                if m >= group:
                    continue
                for dc in range(nco):
                    go(m, lax.rem(rr + r, nr), dc)

        for dr in range(nr):
            for dc in range(nco):
                if dr or dc:
                    go(0, dr, dc)
        pltpu.make_async_copy(piece((r, ch, co)), spot, sem).start()

    def mix(i):
        pair = i < 2
        group = half_ch if pair else nch
        rows = H // group
        first = 0 if pair else i * rp
        for n in ((0, 1) if pair else (i,)):
            got = gath.at[pl.ds(0, rows), pl.ds(0, C // 2 if pair else C), :]
            pltpu.make_async_copy(got, got, crecv.at[n]).wait()

        for k in range(rows):
            v = dot(weight_ref[...], gath[first + k]) + biasb[...]
            inner = 0.7978845608028654 * (v + 0.044715 * (v * v * v))
            brch[first + k] = (0.5 * v * (1.0 + jnp.tanh(inner))).astype(BF16)


    def give(i, targets, own):
        pair = i < 2
        group = half_ch if pair else nch
        rows = H // group
        first = 0 if pair else i * rp
        tile = half if pair else i

        def piece(pc):
            return brch.at[pl.ds(first, rows), pl.ds(pl.multiple_of(pc * CB, CB), CB), :]

        spot = back.at[tile, pl.ds(lax.rem(ch, group) * rows, rows)]

        for c in targets:
            def send(c=c):
                pltpu.make_async_remote_copy(
                    src_ref=piece(c),
                    dst_ref=spot,
                    send_sem=dsend,
                    recv_sem=drecv.at[tile],
                    device_id=dev(at(0, c, 0)),
                    device_id_type=MESH,
                ).start()

            pl.when(ch != c)(send)

        if own:
            pltpu.make_async_copy(piece(ch), spot, drecv.at[tile]).start()

    def finish(t):
        pltpu.make_async_copy(back.at[t], back.at[t], drecv.at[t]).wait()
        for g in range(CB // 16):
            rows = back[t, :, g * 16 : (g + 1) * 16, :].reshape(H * 16, W)
            branch = dot(swap[...], rows).reshape(16, H, W)
            out_ref[t, g * 16 : (g + 1) * 16] = (
                feat[t, g * 16 : (g + 1) * 16].astype(F32) + branch
            ).astype(BF16)

    conv(2)
    push(2)
    constants()
    conv(3)
    push(3)
    conv(0)
    push(0)
    conv(4)
    push(4)
    prepare_mirror()
    conv(1)
    push(1)
    mix(2)
    give(2, (0, 1, 2, 3, 4, 5, 6, 7), True)
    mix(3)
    give(3, (0, 1, 2, 3, 4, 5, 6, 7), True)
    mix(0)
    give(0, (0, 1, 4, 5, 6, 7), True)

    @pl.when(r == 1)
    def _():
        give(0, (2, 3), False)

    mix(4)
    give(4, (0, 1, 4, 5, 6, 7), True)

    @pl.when(r == 1)
    def _():
        give(4, (2, 3), False)


    @pl.when(r == 0)
    def _():
        give(0, (2, 3), False)


    @pl.when(r == 0)
    def _():
        give(4, (2, 3), False)

    own.wait()
    finish(2)
    finish(3)
    finish(0)
    finish(1)
    finish(4)

    sent = whole.at[pl.ds(0, T - 1), :, :, pl.ds(0, cq // quads * (quads - 1))]
    pltpu.make_async_copy(sent, sent, asend.at[0]).wait()
    pltpu.make_async_copy(whole.at[1], whole.at[1], asend.at[1]).wait()
    for k, ref in enumerate((mtapx, mtapy)):
        pltpu.make_async_copy(ref, ref, tsend.at[k]).wait()
    parts = nr * nch * nco
    sent = gath.at[pl.ds(2 * rp, (T - 2) * rp), pl.ds(0, C // parts * (parts - 1)), :]
    pltpu.make_async_copy(sent, sent, csend.at[0]).wait()
    parts = nr * half_ch * nco
    sent = gath.at[pl.ds(0, 2 * rp), pl.ds(0, C // parts * (parts - 1)), :]
    pltpu.make_async_copy(sent, sent, csend.at[1]).wait()
    sent = brch.at[:, pl.ds(0, C // nch * (nch - 1)), :]
    pltpu.make_async_copy(sent, sent, dsend).wait()


def per_device(mesh, feature_map, taps_x, taps_y, mix_weight, mix_bias):
    T, CB, H, W = feature_map.shape
    C = mix_weight.shape[0]
    nr, nch, nco = (mesh.shape[a] for a in ("rows", "chans", "cols"))
    quads = nr * nco
    cq = CB // quads
    rp = H // max(nch, 1)
    FH, FW = nr * H, nco * W
    dims = (T, nr, nch, nco, C, CB, H, W)
    return pl.pallas_call(
        functools.partial(section_kernel, dims),
        out_shape=jax.ShapeDtypeStruct(feature_map.shape, BF16),
        in_specs=[pl.BlockSpec(memory_space=pltpu.HBM)] * 5,
        out_specs=pl.BlockSpec(memory_space=pltpu.VMEM),
        scratch_shapes=[
            pltpu.VMEM(taps_x.shape, BF16),
            pltpu.VMEM(taps_y.shape, BF16),
            pltpu.VMEM(mix_weight.shape, BF16),
            pltpu.VMEM((C,), BF16),
            pltpu.VMEM((T, CB, H, W), BF16),
            pltpu.VMEM((T, nr, nco, cq, H, W), BF16),
            pltpu.VMEM((2, cq, FW, FW), BF16),
            pltpu.VMEM((2, FH * cq, cq * FH), BF16),
            pltpu.VMEM((16 * H, 16 * H), BF16),
            pltpu.VMEM((C, W), F32),
            pltpu.VMEM((cq * FH, FW), BF16),
            pltpu.VMEM((T, nco, FH, cq, W), BF16),
            pltpu.VMEM((T * rp, C, W), BF16),
            pltpu.VMEM((T * rp, C, W), BF16),
            pltpu.VMEM((T, H, CB, W), BF16),
            pltpu.VMEM((cq, KERNEL_TAPS), BF16),
            pltpu.VMEM((cq, KERNEL_TAPS), BF16),
            pltpu.SemaphoreType.DMA((5 + T,)),
            pltpu.SemaphoreType.DMA((2,)),
            pltpu.SemaphoreType.DMA((T,)),
            pltpu.SemaphoreType.DMA((2,)),
            pltpu.SemaphoreType.DMA((T,)),
            pltpu.SemaphoreType.DMA,
            pltpu.SemaphoreType.DMA((T,)),
            pltpu.SemaphoreType.DMA((2,)),
            pltpu.SemaphoreType.DMA((2,)),
            pltpu.SemaphoreType.REGULAR((3,)),
            pltpu.SemaphoreType.REGULAR((4 + 2,)),
        ],
        compiler_params=pltpu.CompilerParams(
            collective_id=0, has_side_effects=True, vmem_limit_bytes=40 * 1024 * 1024
        ),
    )(*(pltpu.with_memory_space_constraint(v, pltpu.HBM) for v in (feature_map, taps_x, taps_y, mix_weight, mix_bias)))


def fits_kernel(mesh):
    return mesh.shape["rows"] == 2 and mesh.shape["cols"] == 2 and mesh.shape["chans"] == 8


def solution(mesh):
    body = functools.partial(per_device, mesh) if fits_kernel(mesh) else per_device_general
    return jax.shard_map(
        body,
        mesh=mesh,
        in_specs=(
            P("groups", "chans", "rows", "cols"),
            P("chans", None),
            P("chans", None),
            P(),
            P(),
        ),
        out_specs=P("groups", "chans", "rows", "cols"),
        check_vma=False,
    )
```
